32 devices in a mesh: expert: 4 (over y, x), tensor: 8 (over z, core).
Axes of the slice: x: 2, y: 2, z: 4, core: 2. Of those that a mesh axis runs over, the one named last changes fastest.
Arguments:
- tokens: bfloat16 [512, 7168], P('expert', 'tensor'), may hold values from -6 to 6
- gate_weights: bfloat16 [512, 1], P('expert'), may hold values from 0.099609375 to 1
- expert_ids: int32 [512, 1], P('expert'), may hold values from 0 to 3; in each aligned block of 128 rows (0 to 127, 128 to 255, ...) at most 48 rows name the same one
- w_gate: bfloat16 [4, 7168, 2048], P('expert', 'tensor'), may hold values from -0.0625 to 0.0625
- w_up: bfloat16 [4, 7168, 2048], P('expert', 'tensor'), may hold values from -0.0625 to 0.0625
- w_down: bfloat16 [4, 2048, 7168], P('expert', None, 'tensor'), may hold values from -0.125 to 0.125
- grad_out: bfloat16 [512, 7168], P('expert', 'tensor'), may hold values from -6 to 6
Outputs:
- mixed: bfloat16 [512, 7168], P('expert', 'tensor')
- grad_tokens: bfloat16 [512, 7168], P('expert', 'tensor')
- grad_w_gate: bfloat16 [4, 7168, 2048], P('expert', 'tensor')
- grad_w_up: bfloat16 [4, 7168, 2048], P('expert', 'tensor')
- grad_w_down: bfloat16 [4, 2048, 7168], P('expert', None, 'tensor')
The draws below stay inside these ranges and needn't reach their ends.
Inputs may be any that keep to these rules, and one draw needn't show every extreme that they name: `expert_ids`: the 1 expert of a token differ. The tokens of one expert index (aligned blocks of 128 rows) name one expert at most 48 times, a bound that some block reaches.
All inputs are finite; a program needn't handle non-finite values.
Results may differ from the reference program's by a relative error of at most 0.0058.
Values may be sent and summed in bfloat16 or wider, within the bound.
No kernel may reach another device: no remote copies, remote signals or barrier semaphores. Data moves between devices by JAX's collectives and lax.ppermute only.
A program may use at most 64 MiB of HBM per device.

```python
import math
import jax
import jax.numpy as jnp
import numpy as np
from jax import lax

D = 7168
FF = 2048
TOPK = 1
TOK_G = 128
EXPERTS = 4
SLOT = 48
ROWS = 192
TOKENS = 512


def block_levels(own_key, dims, split, low, top_value):
    def one(position, parts):
        draws = jax.random.uniform(jax.random.fold_in(jax.random.fold_in(own_key, 6), position), (parts,), jnp.float32, low / len(split), top_value / len(split))
        return jnp.repeat(jnp.exp(draws), dims[position] // parts).reshape((-1,) + (1,) * (len(dims) - position - 1))

    level = one(*split[0])
    for cut in split[1:]:
        level = level * one(*cut)
    return level


def routed_block(rng, own, number, rows, count, top, bound, lean):
    sequence = jax.random.permutation(rng, count)
    heavy_load, common = portions_of(count, rows * top, bound, lean, True), portions_of(count, rows * top, bound, lean, False)
    places = jnp.arange(count)

    def named(tallies, offset_by):
        used = int((tallies > 0).sum())
        fixed = max(1, used // 4)
        passed = fixed + (places - fixed + offset_by * (used - fixed)) % max(1, count - fixed)
        return jnp.zeros((count,), jnp.int32).at[sequence[jnp.where(places < fixed, places, passed)]].set(jnp.asarray(tallies, jnp.int32))

    tallies = jnp.where(number % 4 == 0, named(heavy_load, number // 4), named(common, number - number // 4 - 1))
    mixed = jax.random.permutation(jax.random.fold_in(own, 3), count)
    donor, sink = mixed[0:count // 2 * 2:2], mixed[1:count // 2 * 2:2]
    margin = jnp.minimum(tallies[donor] - 1, bound - tallies[sink]) // 2
    margin = jnp.where((donor == sequence[0]) | (sink == sequence[0]) | (tallies[sink] == 0), 0, jnp.maximum(margin, 0))
    passed = jax.random.randint(jax.random.fold_in(own, 4), (count // 2,), 0, 1 << 20) % (margin + 1)
    tallies = tallies.at[donor].add(-passed).at[sink].add(passed)
    items = jnp.searchsorted(jnp.cumsum(tallies), jnp.arange(rows * top), side="right").astype(jnp.int32)
    table = items.reshape(top, rows).T
    table = table[jax.random.permutation(jax.random.fold_in(own, 1), rows)]
    offset_by = jax.random.randint(jax.random.fold_in(own, 2), (rows, 1), 0, top)
    return jnp.take_along_axis(table, (jnp.arange(top)[None, :] + offset_by) % top, axis=1)


def portions_of(count, total, most, slope, full):
    loads = [(1 << 20) // math.isqrt(grade ** slope) + 1 for grade in range(1, count + 1)]
    largest = most if full else min(most, max(-(-total // count), total * loads[0] // sum(loads)))
    least = 1 if total - largest >= count - 1 else 0
    holding, surplus = [largest] + [least] * (count - 1), total - largest - least * (count - 1)
    while surplus > 0:
        free = [i for i in range(1, count) if holding[i] < largest] or [i for i in range(1, count) if holding[i] < most]
        whole, left = sum([loads[i] for i in free]), surplus
        for i in free:
            addition = min(most - holding[i], max(1, left * loads[i] // whole), surplus)
            holding[i] = holding[i] + addition
            surplus = surplus - addition
    return np.array(holding)


def scatter_about(rng, dims, width, reach, cuts=(), kind=jnp.bfloat16):
    values = jax.random.normal(rng, dims, jnp.float32) * width
    if len(cuts) > 0:
        values = block_levels(rng, dims, cuts, -0.22, 0.18) * values
    return jnp.clip(values, min=-reach, max=reach).astype(kind)


def setup_inputs(seed: int = 0) -> dict:
    key_list = jax.random.split(jax.random.key(seed), 8)
    tokens = scatter_about(key_list[0], (TOKENS, D), 1.0, 6.0, ((0, 4), (1, 8)))
    gate_weights = jnp.clip(0.099609375 + 0.9003906 * jax.random.uniform(key_list[1], (TOKENS, TOPK), jnp.float32) ** block_levels(key_list[1], (TOKENS, TOPK), ((0, 4),), -0.2, 0.2), 0.099609375, 1.0).astype(jnp.bfloat16)
    expert_ids_keys = jax.random.split(jax.random.fold_in(key_list[2], 1), TOKENS // TOK_G)
    expert_ids_turns = jax.random.permutation(jax.random.fold_in(key_list[2], 3), TOKENS // TOK_G)
    expert_ids = jax.vmap(lambda own, number: routed_block(jax.random.fold_in(key_list[2], 2), own, number, TOK_G, EXPERTS, TOPK, SLOT, 2))(expert_ids_keys, expert_ids_turns).reshape((TOKENS, TOPK))
    w_gate = scatter_about(key_list[3], (EXPERTS, D, FF), D ** -0.5, 0.0625, ((0, 4), (1, 8)))
    w_up = scatter_about(key_list[4], (EXPERTS, D, FF), D ** -0.5, 0.0625, ((0, 4), (1, 8)))
    w_down = scatter_about(key_list[5], (EXPERTS, FF, D), FF ** -0.5, 0.125, ((0, 4), (2, 8)))
    grad_out = scatter_about(key_list[6], (TOKENS, D), 1.0, 6.0, ((0, 4), (1, 8)))
    return dict(tokens=tokens, gate_weights=gate_weights, expert_ids=expert_ids, w_gate=w_gate, w_up=w_up, w_down=w_down, grad_out=grad_out)


def reference(tokens, gate_weights, expert_ids, w_gate, w_up, w_down, grad_out):
    flat_ids = expert_ids.reshape(-1).astype(jnp.int32)
    flat_gate = gate_weights.reshape(-1)
    route_token = (jnp.arange(flat_ids.shape[0], dtype=jnp.int32) // TOPK).astype(jnp.int32)

    def one_expert(packed):
        weight_gate, weight_up, weight_down, index = packed
        chosen = flat_ids == index
        picks = jnp.nonzero(chosen, size=ROWS, fill_value=0)[0].astype(jnp.int32)
        live = (jnp.arange(ROWS, dtype=jnp.int32) < jnp.sum(chosen.astype(jnp.int32))).astype(jnp.float32)
        token_index = route_token[picks]
        weight = flat_gate[picks].astype(jnp.float32) * live
        x_rows = tokens[token_index]
        gate = jnp.dot(x_rows, weight_gate, preferred_element_type=jnp.float32)
        up = jnp.dot(x_rows, weight_up, preferred_element_type=jnp.float32)
        sigma = jax.nn.sigmoid(gate)
        active = gate * sigma
        hidden = (active * up).astype(jnp.bfloat16)
        expert_out = jnp.dot(hidden, weight_down, preferred_element_type=jnp.float32).astype(jnp.bfloat16)
        scaled = (weight[:, None] * grad_out[token_index].astype(jnp.float32)).astype(jnp.bfloat16)
        d_hidden = jnp.dot(scaled, weight_down.T, preferred_element_type=jnp.float32)
        d_gate = (d_hidden * up * sigma * (1.0 + gate * (1.0 - sigma))).astype(jnp.bfloat16)
        d_up = (d_hidden * active).astype(jnp.bfloat16)
        route_grad = (jnp.dot(d_gate, weight_gate.T, preferred_element_type=jnp.float32)
                      + jnp.dot(d_up, weight_up.T, preferred_element_type=jnp.float32)).astype(jnp.bfloat16)
        grad_gate = jnp.dot(x_rows.T, d_gate, preferred_element_type=jnp.float32).astype(jnp.bfloat16)
        grad_up = jnp.dot(x_rows.T, d_up, preferred_element_type=jnp.float32).astype(jnp.bfloat16)
        grad_down = jnp.dot(hidden.T, scaled, preferred_element_type=jnp.float32).astype(jnp.bfloat16)
        return expert_out, route_grad, token_index, weight, live, grad_gate, grad_up, grad_down

    indices = jnp.arange(EXPERTS, dtype=jnp.int32)
    outs = lax.map(one_expert, (w_gate, w_up, w_down, indices))
    expert_out, route_grad, token_index, weight, live, grad_w_gate, grad_w_up, grad_w_down = outs
    flat_index = token_index.reshape(-1)
    mixed_terms = (weight[:, :, None] * expert_out.astype(jnp.float32)).reshape(-1, D)
    mixed = jax.ops.segment_sum(mixed_terms, flat_index, num_segments=TOKENS).astype(jnp.bfloat16)
    grad_terms = (live[:, :, None] * route_grad.astype(jnp.float32)).reshape(-1, D)
    grad_tokens = jax.ops.segment_sum(grad_terms, flat_index, num_segments=TOKENS).astype(jnp.bfloat16)
    return mixed, grad_tokens, grad_w_gate, grad_w_up, grad_w_down
```

```python
import functools

import jax
import jax.numpy as jnp
from jax import lax
from jax.experimental import pallas as pl
from jax.experimental.pallas import tpu as pltpu
from jax.sharding import PartitionSpec as P

F32 = jnp.float32
BF16 = jnp.bfloat16


def spread_units(function):
    return lax.psum_scatter(function(), "tensor", scatter_dimension=0, tiled=True)


def general(tokens, gate_weights, expert_ids, w_gate, w_up, w_down, grad_out):
    members = lax.axis_size("expert")
    tok_rows = tokens.shape[0]
    routes = expert_ids.shape[1]
    width = tokens.shape[1]
    slot = 3 * routes * tok_rows // (2 * members)
    total = members * slot
    flat_ids = expert_ids.reshape(-1)
    counted = (flat_ids[:, None] == jnp.arange(members, dtype=jnp.int32)[None, :]).astype(jnp.int32)
    ranks = jnp.cumsum(counted, axis=0) - 1
    position = jnp.sum(counted * ranks, axis=1)
    target = (flat_ids * slot + position).reshape(tok_rows, routes)
    matched = target[None, :, :] == jnp.arange(total, dtype=jnp.int32)[:, None, None]
    place = jnp.sum(matched.astype(F32), axis=2).astype(BF16)
    weighted = jnp.sum(jnp.where(matched, gate_weights.astype(F32)[None], 0.0), axis=2).astype(BF16)
    x_slots = jnp.dot(place, tokens, preferred_element_type=F32).astype(BF16)
    dy_slots = jnp.dot(weighted, grad_out, preferred_element_type=F32).astype(BF16)
    outgoing = jnp.stack(
        [x_slots.reshape(members, slot, width), dy_slots.reshape(members, slot, width)], axis=1
    )
    arrived = lax.all_to_all(outgoing, "expert", split_axis=0, concat_axis=0, tiled=True)
    x_rows = arrived[:, 0].reshape(total, width)
    dy_rows = arrived[:, 1].reshape(total, width)
    weight_gate, weight_up, weight_down = w_gate[0], w_up[0], w_down[0]
    dot = functools.partial(lax.dot_general, preferred_element_type=F32)

    def gate_terms():
        return jnp.concatenate(
            [dot(w, x_rows, (((0,), (1,)), ((), ()))) for w in (weight_gate, weight_up)], axis=1
        )

    summed = spread_units(gate_terms)
    gate_t, up_t = summed[:, :total], summed[:, total:]
    sigma = jax.nn.sigmoid(gate_t)
    active = gate_t * sigma
    hidden_t = (active * up_t).astype(BF16)
    hidden = lax.all_gather(hidden_t, "tensor", axis=0, tiled=True)
    out_rows = dot(hidden, weight_down, (((0,), (0,)), ((), ()))).astype(BF16)
    swap = functools.partial(
        lax.all_to_all, axis_name="expert", split_axis=0, concat_axis=0, tiled=True
    )
    out_back = swap(out_rows.reshape(members, slot, width))
    d_hidden = spread_units(lambda: dot(weight_down, dy_rows, (((1,), (1,)), ((), ()))))
    d_gate_t = (d_hidden * up_t * sigma * (1.0 + gate_t * (1.0 - sigma))).astype(BF16)
    d_up_t = (d_hidden * active).astype(BF16)
    d_gate = lax.all_gather(d_gate_t, "tensor", axis=0, tiled=True)
    d_up = lax.all_gather(d_up_t, "tensor", axis=0, tiled=True)
    back_rows = (
        dot(d_gate, weight_gate, (((0,), (1,)), ((), ())))
        + dot(d_up, weight_up, (((0,), (1,)), ((), ())))
    ).astype(BF16)
    grad_w_gate = dot(x_rows, d_gate, (((0,), (1,)), ((), ()))).astype(BF16)[None]
    grad_w_up = dot(x_rows, d_up, (((0,), (1,)), ((), ()))).astype(BF16)[None]
    grad_w_down = dot(hidden, dy_rows, (((1,), (0,)), ((), ()))).astype(BF16)[None]
    grad_back = swap(back_rows.reshape(members, slot, width))
    mixed = dot(weighted, out_back.reshape(total, width), (((0,), (0,)), ((), ()))).astype(BF16)
    grad_tokens = dot(place, grad_back.reshape(total, width), (((0,), (0,)), ((), ()))).astype(BF16)
    return (mixed, grad_tokens, grad_w_gate, grad_w_up, grad_w_down)


NT = (((1,), (1,)), ((), ()))
TN = (((0,), (0,)), ((), ()))
NN = (((1,), (0,)), ((), ()))


def mm(a, b, dims=NN):
    return lax.dot_general(a, b, dims, preferred_element_type=F32)


def params(mib=24):
    return pltpu.CompilerParams(vmem_limit_bytes=mib * 2**20)


def cost(flops, nbytes):
    return pl.CostEstimate(flops=int(flops), bytes_accessed=int(nbytes), transcendentals=0)


def placement(ids, here, members, slot, total):
    count = ids.shape[1]
    lanes = lax.broadcasted_iota(jnp.int32, (max(members, 8), count), 0)
    chosen = (lanes == ids).astype(F32)
    before = lax.broadcasted_iota(jnp.int32, (count, count), 0) < lax.broadcasted_iota(
        jnp.int32, (count, count), 1
    )
    ranks = mm(chosen.astype(BF16), before.astype(F32).astype(BF16))
    rank = jnp.sum(chosen * ranks, axis=0, keepdims=True).astype(jnp.int32)
    target = (ids ^ here) * slot + rank
    return lax.broadcasted_iota(jnp.int32, (total, count), 0) == target


def dispatch(ids, here, data, gates, members, slot):
    total, width = members * slot, data.shape[1]

    def kernel(here_ref, ids_ref, *refs):
        data_ref, out_refs = refs[-members - 1], refs[-members:]
        mask = placement(ids_ref[...], here_ref[0], members, slot, total)
        value = 1.0 if gates is None else refs[0][...].astype(F32)
        rows = mm(jnp.where(mask, value, 0.0).astype(BF16), data_ref[...]).astype(BF16)
        for m, ref in enumerate(out_refs):
            ref[...] = rows[m * slot : (m + 1) * slot]

    vmem = pl.BlockSpec(memory_space=pltpu.VMEM)
    extra = () if gates is None else (gates,)
    return pl.pallas_call(
        kernel,
        out_shape=[jax.ShapeDtypeStruct((slot, width), BF16)] * members,
        in_specs=[pl.BlockSpec(memory_space=pltpu.SMEM), vmem] + [vmem] * len(extra) + [vmem],
        out_specs=[vmem] * members,
        compiler_params=params(8),
        cost_estimate=cost(2 * total * data.size, 4 * data.size),
        name="dispatch",
    )(here, ids, *extra, data)


def collect(ids, here, rows, gates, members, slot):
    total, width, count = members * slot, rows[0].shape[1], ids.shape[1]

    def kernel(here_ref, ids_ref, *refs):
        row_refs, out_ref, joined = refs[-members - 2 : -2], refs[-2], refs[-1]
        for m, ref in enumerate(row_refs):
            joined[m * slot : (m + 1) * slot, :] = ref[...]
        mask = placement(ids_ref[...], here_ref[0], members, slot, total)
        value = 1.0 if gates is None else refs[0][...].astype(F32)
        pick = jnp.where(mask, value, 0.0).astype(BF16)
        out_ref[...] = mm(pick, joined[...], TN).astype(BF16)

    vmem = pl.BlockSpec(memory_space=pltpu.VMEM)
    extra = () if gates is None else (gates,)
    return pl.pallas_call(
        kernel,
        out_shape=jax.ShapeDtypeStruct((count, width), BF16),
        in_specs=[pl.BlockSpec(memory_space=pltpu.SMEM), vmem] + [vmem] * (len(extra) + members),
        out_specs=vmem,
        scratch_shapes=[pltpu.VMEM((total, width), BF16)],
        compiler_params=params(8),
        cost_estimate=cost(2 * count * total * width, 4 * total * width),
        name="collect",
    )(here, ids, *extra, *rows)


def partial_units(order, rows, weights, unit, down, kept=None, first=0):
    members, slot, width = len(rows), rows[0].shape[0], rows[0].shape[1]
    total, n, blocks = members * slot, len(weights), order.shape[0]

    def kernel(order_ref, *refs):
        row_refs, w_refs = refs[:members], refs[members : members + n]
        rest, joined = refs[members + n : -1], refs[-1]
        j = pl.program_id(0)

        @pl.when(j == 0)
        def _():
            for m, ref in enumerate(row_refs):
                joined[m * slot : (m + 1) * slot, :] = ref[...]

        for i, w_ref in enumerate(w_refs):
            term = mm(joined[...], w_ref[...], NT if down else NN)
            if kept is None:
                rest[0][0, i] = term.astype(BF16)
            else:
                term = term + rest[0][0, i].astype(F32)

                @pl.when(j < first)
                def _():
                    rest[1][0, i] = term.astype(BF16)

                @pl.when(j >= first)
                def _():
                    rest[2][0, i] = term

    whole = pl.BlockSpec((slot, width), lambda j, o: (0, 0))
    w_spec = (
        pl.BlockSpec((unit, width), lambda j, o: (o[j], 0))
        if down
        else pl.BlockSpec((width, unit), lambda j, o: (0, o[j]))
    )
    block = (1, n, total, unit)
    if kept is None:
        extra, extra_specs = (), []
        shapes = [jax.ShapeDtypeStruct((blocks, n, total, unit), BF16)]
        out_specs = [pl.BlockSpec(block, lambda j, o: (j, 0, 0, 0))]
    else:
        extra = (kept,)
        extra_specs = [pl.BlockSpec(block, lambda j, o: ((j + first) % blocks, 0, 0, 0))]
        shapes = [
            jax.ShapeDtypeStruct((first, n, total, unit), BF16),
            jax.ShapeDtypeStruct((blocks - first, n, total, unit), F32),
        ]
        out_specs = [
            pl.BlockSpec(block, lambda j, o: (jnp.minimum(j, first - 1), 0, 0, 0)),
            pl.BlockSpec(block, lambda j, o: (jnp.maximum(j - first, 0), 0, 0, 0)),
        ]
    return pl.pallas_call(
        kernel,
        out_shape=shapes,
        grid_spec=pltpu.PrefetchScalarGridSpec(
            num_scalar_prefetch=1,
            grid=(blocks,),
            in_specs=[whole] * members + [w_spec] * n + extra_specs,
            out_specs=out_specs,
            scratch_shapes=[pltpu.VMEM((total, width), BF16)],
        ),
        compiler_params=params(),
        cost_estimate=cost(
            2 * n * blocks * total * width * unit, 2 * n * blocks * unit * (width + 2 * total)
        ),
        name="partial_units",
    )(order, *rows, *weights)[0] if kept is None else pl.pallas_call(
        kernel,
        out_shape=shapes,
        grid_spec=pltpu.PrefetchScalarGridSpec(
            num_scalar_prefetch=1,
            grid=(blocks,),
            in_specs=[whole] * members + [w_spec] * n + extra_specs,
            out_specs=out_specs,
            scratch_shapes=[pltpu.VMEM((total, width), BF16)],
        ),
        compiler_params=params(),
        cost_estimate=cost(
            2 * n * blocks * total * width * unit, 2 * n * blocks * unit * (width + 4 * total)
        ),
        name="partial_units",
    )(order, *rows, *weights, *extra)


def full_units(order, pieces, weights, slot, unit, down):
    n, total = pieces[0].shape[1], pieces[0].shape[2]
    width = weights[0].shape[1] if down else weights[0].shape[0]
    members, blocks = total // slot, order.shape[0]
    starts = [sum(p.shape[0] for p in pieces[:i]) for i in range(len(pieces))]

    def kernel(order_ref, *refs):
        piece_refs, w_refs = refs[: len(pieces)], refs[len(pieces) : len(pieces) + n]
        out_refs, acc = refs[len(pieces) + n : -1], refs[-1]
        j = pl.program_id(0)

        @pl.when(j == 0)
        def _():
            acc[...] = jnp.zeros_like(acc)

        for p, ref in enumerate(piece_refs):

            @pl.when((j >= starts[p]) & (j < starts[p] + pieces[p].shape[0]))
            def _():
                term = mm(ref[0, 0], w_refs[0][...], NN if down else NT)
                for i in range(1, n):
                    term = term + mm(ref[0, i], w_refs[i][...], NN if down else NT)
                acc[...] += term

        @pl.when(j == blocks - 1)
        def _():
            for m, ref in enumerate(out_refs):
                ref[...] = acc[m * slot : (m + 1) * slot, :].astype(BF16)

    w_spec = (
        pl.BlockSpec((unit, width), lambda j, o: (o[j], 0))
        if down
        else pl.BlockSpec((width, unit), lambda j, o: (0, o[j]))
    )
    return pl.pallas_call(
        kernel,
        out_shape=[jax.ShapeDtypeStruct((slot, width), BF16)] * members,
        grid_spec=pltpu.PrefetchScalarGridSpec(
            num_scalar_prefetch=1,
            grid=(blocks,),
            in_specs=[piece_spec(p, s, total, unit) for p, s in zip(pieces, starts)]
            + [w_spec] * n,
            out_specs=[pl.BlockSpec((slot, width), lambda j, o: (0, 0))] * members,
            scratch_shapes=[pltpu.VMEM((total, width), F32)],
        ),
        compiler_params=params(),
        cost_estimate=cost(
            2 * n * blocks * total * width * unit, 2 * n * blocks * unit * (width + total)
        ),
        name="full_units",
    )(order, *pieces, *weights)


def piece_spec(piece, start, total, unit):
    last = piece.shape[0] - 1
    return pl.BlockSpec(
        (1, piece.shape[1], total, unit),
        lambda j, o: (jnp.clip(j - start, 0, last), 0, 0, 0),
    )


def weight_grads(order, pieces, rows, unit, down):
    n, total = pieces[0].shape[1], pieces[0].shape[2]
    members, slot, width = len(rows), rows[0].shape[0], rows[0].shape[1]
    blocks = order.shape[0]
    starts = [sum(p.shape[0] for p in pieces[:i]) for i in range(len(pieces))]

    def kernel(order_ref, *refs):
        piece_refs, row_refs = refs[: len(pieces)], refs[len(pieces) : len(pieces) + members]
        out_refs, joined = refs[len(pieces) + members : -1], refs[-1]
        j = pl.program_id(0)

        @pl.when(j == 0)
        def _():
            for m, ref in enumerate(row_refs):
                joined[m * slot : (m + 1) * slot, :] = ref[...]

        for p, ref in enumerate(piece_refs):

            @pl.when((j >= starts[p]) & (j < starts[p] + pieces[p].shape[0]))
            def _():
                for i, out_ref in enumerate(out_refs):
                    if down:
                        out_ref[0] = mm(ref[0, i], joined[...], TN).astype(BF16)
                    else:
                        out_ref[0] = mm(joined[...], ref[0, i], TN).astype(BF16)

    whole = pl.BlockSpec((slot, width), lambda j, o: (0, 0))
    if down:
        shape = (1, blocks * unit, width)
        out_spec = pl.BlockSpec((1, unit, width), lambda j, o: (0, o[j], 0))
    else:
        shape = (1, width, blocks * unit)
        out_spec = pl.BlockSpec((1, width, unit), lambda j, o: (0, 0, o[j]))
    return pl.pallas_call(
        kernel,
        out_shape=[jax.ShapeDtypeStruct(shape, BF16)] * n,
        grid_spec=pltpu.PrefetchScalarGridSpec(
            num_scalar_prefetch=1,
            grid=(blocks,),
            in_specs=[piece_spec(p, s, total, unit) for p, s in zip(pieces, starts)]
            + [whole] * members,
            out_specs=[out_spec] * n,
            scratch_shapes=[pltpu.VMEM((total, width), BF16)],
        ),
        compiler_params=params(),
        cost_estimate=cost(
            2 * n * blocks * total * width * unit, 2 * n * blocks * unit * (width + total)
        ),
        name="weight_grads",
    )(order, *pieces, *rows)


def hypercube(tokens, gate_weights, expert_ids, w_gate, w_up, w_down, grad_out):
    members = lax.axis_size("expert")
    parts = lax.axis_size("tensor")
    bits = (parts // 2).bit_length() - 1
    count = tokens.shape[0]
    slot = 3 * count // (2 * members)
    weight_gate, weight_up, weight_down = w_gate[0], w_up[0], w_down[0]
    unit = weight_gate.shape[1] // parts
    half = parts // 2

    own = lax.axis_index("expert")
    here = own.reshape(1)
    ids = expert_ids.reshape(1, count)
    gates = gate_weights.reshape(1, count)

    t = lax.axis_index("tensor")
    core, chip = t % 2, t // 2
    orders = (tuple(range(bits)), tuple(reversed(range(bits))))

    def pairs(step):
        return [(d, d ^ (2 << orders[d % 2][step])) for d in range(parts)]

    def step_swap(x, step):
        return lax.ppermute(x, "tensor", pairs(step))

    def core_swap(x):
        return lax.ppermute(x, "tensor", [(d, d ^ 1) for d in range(parts)])

    def block_ids(c):
        out = []
        for rel in range(half):
            place = [jnp.int32(0), jnp.int32(0)]
            for k in range(2):
                for step in range(bits):
                    bit = (chip >> orders[k][step]) & 1
                    flip = (rel >> (bits - 1 - step)) & 1
                    place[k] = place[k] * 2 + (bit ^ flip)
            out.append(half * c + jnp.where(c == 0, place[0], place[1]))
        return jnp.stack(out).astype(jnp.int32)

    mine, other = block_ids(core), block_ids(1 - core)
    first = half // 2
    send_first = jnp.concatenate([mine[first:], mine[:first]])
    every = jnp.concatenate([mine, other])

    def expert_swap(rows):
        return [rows[0]] + [
            lax.ppermute(rows[m], "expert", [(d, d ^ m) for d in range(members)])
            for m in range(1, members)
        ]

    def reduce_units(rows, weights, down):
        away = partial_units(other, rows, weights, unit, down)
        arrived = core_swap(away)
        send, keep = partial_units(send_first, rows, weights, unit, down, arrived, first)
        size = first
        for step in range(bits):
            got = step_swap(send, step)
            total = keep + got.astype(F32)
            size //= 2
            if step < bits - 1:
                send, keep = total[size:].astype(BF16), total[:size]
        return total[0]

    def gather_units(x):
        for step in reversed(range(bits)):
            x = jnp.concatenate([x, step_swap(x, step)], axis=0)
        return [x, core_swap(x)]

    x_rows = expert_swap(dispatch(ids, here, tokens, None, members, slot))
    dy_rows = expert_swap(dispatch(ids, here, grad_out, gates, members, slot))

    gate, up = reduce_units(x_rows, (weight_gate, weight_up), False)
    (d_hidden,) = reduce_units(dy_rows, (weight_down,), True)

    sigma = jax.nn.sigmoid(gate)
    active = gate * sigma
    hidden = (active * up).astype(BF16)
    d_gate = (d_hidden * up * sigma * (1.0 + gate * (1.0 - sigma))).astype(BF16)
    d_up = (d_hidden * active).astype(BF16)

    hidden_all = gather_units(hidden[None, None])
    out_rows = full_units(every, hidden_all, (weight_down,), slot, unit, True)
    out_back = expert_swap(out_rows)
    (grad_w_down,) = weight_grads(every, hidden_all, dy_rows, unit, True)

    d_all = gather_units(jnp.stack([d_gate, d_up])[None])
    back_rows = full_units(every, d_all, (weight_gate, weight_up), slot, unit, False)
    grad_back = expert_swap(back_rows)
    grad_w_gate, grad_w_up = weight_grads(every, d_all, x_rows, unit, False)

    mixed = collect(ids, here, out_back, gates, members, slot)
    grad_tokens = collect(ids, here, grad_back, None, members, slot)
    return (mixed, grad_tokens, grad_w_gate, grad_w_up, grad_w_down)


def power_of_two(n):
    return n & (n - 1) == 0


def solution(mesh):
    members, parts = mesh.shape["expert"], mesh.shape["tensor"]

    def local(*args):
        unit = args[3].shape[2] // parts
        slot = 3 * args[0].shape[0] // (2 * members)
        fits = power_of_two(members) and power_of_two(parts) and parts >= 4
        fits = fits and unit % 128 == 0 and slot % 16 == 0 and args[0].shape[1] % 128 == 0
        fits = fits and args[2].shape[1] == 1
        return (hypercube if fits else general)(*args)

    in_specs = (
        P("expert", "tensor"),
        P("expert", None),
        P("expert", None),
        P("expert", "tensor", None),
        P("expert", "tensor", None),
        P("expert", None, "tensor"),
        P("expert", "tensor"),
    )
    out_specs = (
        P("expert", "tensor"),
        P("expert", "tensor"),
        P("expert", "tensor", None),
        P("expert", "tensor", None),
        P("expert", None, "tensor"),
    )
    return jax.shard_map(local, mesh=mesh, in_specs=in_specs, out_specs=out_specs, check_vma=False)
```

```python
import functools

import jax
import jax.numpy as jnp
from jax import lax
from jax.experimental import pallas as pl
from jax.experimental.pallas import tpu as pltpu
from jax.sharding import PartitionSpec as P

F32 = jnp.float32
BF16 = jnp.bfloat16


def spread_units(function):
    return lax.psum_scatter(function(), "tensor", scatter_dimension=0, tiled=True)


def general(tokens, gate_weights, expert_ids, w_gate, w_up, w_down, grad_out):
    members = lax.axis_size("expert")
    tok_rows = tokens.shape[0]
    routes = expert_ids.shape[1]
    width = tokens.shape[1]
    slot = 3 * routes * tok_rows // (2 * members)
    total = members * slot
    flat_ids = expert_ids.reshape(-1)
    counted = (flat_ids[:, None] == jnp.arange(members, dtype=jnp.int32)[None, :]).astype(jnp.int32)
    ranks = jnp.cumsum(counted, axis=0) - 1
    position = jnp.sum(counted * ranks, axis=1)
    target = (flat_ids * slot + position).reshape(tok_rows, routes)
    matched = target[None, :, :] == jnp.arange(total, dtype=jnp.int32)[:, None, None]
    place = jnp.sum(matched.astype(F32), axis=2).astype(BF16)
    weighted = jnp.sum(jnp.where(matched, gate_weights.astype(F32)[None], 0.0), axis=2).astype(BF16)
    x_slots = jnp.dot(place, tokens, preferred_element_type=F32).astype(BF16)
    dy_slots = jnp.dot(weighted, grad_out, preferred_element_type=F32).astype(BF16)
    outgoing = jnp.stack(
        [x_slots.reshape(members, slot, width), dy_slots.reshape(members, slot, width)], axis=1
    )
    arrived = lax.all_to_all(outgoing, "expert", split_axis=0, concat_axis=0, tiled=True)
    x_rows = arrived[:, 0].reshape(total, width)
    dy_rows = arrived[:, 1].reshape(total, width)
    weight_gate, weight_up, weight_down = w_gate[0], w_up[0], w_down[0]
    dot = functools.partial(lax.dot_general, preferred_element_type=F32)

    def gate_terms():
        return jnp.concatenate(
            [dot(w, x_rows, (((0,), (1,)), ((), ()))) for w in (weight_gate, weight_up)], axis=1
        )

    summed = spread_units(gate_terms)
    gate_t, up_t = summed[:, :total], summed[:, total:]
    sigma = jax.nn.sigmoid(gate_t)
    active = gate_t * sigma
    hidden_t = (active * up_t).astype(BF16)
    hidden = lax.all_gather(hidden_t, "tensor", axis=0, tiled=True)
    out_rows = dot(hidden, weight_down, (((0,), (0,)), ((), ()))).astype(BF16)
    swap = functools.partial(
        lax.all_to_all, axis_name="expert", split_axis=0, concat_axis=0, tiled=True
    )
    out_back = swap(out_rows.reshape(members, slot, width))
    d_hidden = spread_units(lambda: dot(weight_down, dy_rows, (((1,), (1,)), ((), ()))))
    d_gate_t = (d_hidden * up_t * sigma * (1.0 + gate_t * (1.0 - sigma))).astype(BF16)
    d_up_t = (d_hidden * active).astype(BF16)
    d_gate = lax.all_gather(d_gate_t, "tensor", axis=0, tiled=True)
    d_up = lax.all_gather(d_up_t, "tensor", axis=0, tiled=True)
    back_rows = (
        dot(d_gate, weight_gate, (((0,), (1,)), ((), ())))
        + dot(d_up, weight_up, (((0,), (1,)), ((), ())))
    ).astype(BF16)
    grad_w_gate = dot(x_rows, d_gate, (((0,), (1,)), ((), ()))).astype(BF16)[None]
    grad_w_up = dot(x_rows, d_up, (((0,), (1,)), ((), ()))).astype(BF16)[None]
    grad_w_down = dot(hidden, dy_rows, (((1,), (0,)), ((), ()))).astype(BF16)[None]
    grad_back = swap(back_rows.reshape(members, slot, width))
    mixed = dot(weighted, out_back.reshape(total, width), (((0,), (0,)), ((), ()))).astype(BF16)
    grad_tokens = dot(place, grad_back.reshape(total, width), (((0,), (0,)), ((), ()))).astype(BF16)
    return (mixed, grad_tokens, grad_w_gate, grad_w_up, grad_w_down)


NT = (((1,), (1,)), ((), ()))
TN = (((0,), (0,)), ((), ()))
NN = (((1,), (0,)), ((), ()))
VMEM = pl.BlockSpec(memory_space=pltpu.VMEM)
SMEM = pl.BlockSpec(memory_space=pltpu.SMEM)
ANY = pl.BlockSpec(memory_space=pl.ANY)


def mm(a, b, dims=NN):
    return lax.dot_general(a, b, dims, preferred_element_type=F32)


def spec(shape, dtype=BF16):
    return jax.ShapeDtypeStruct(shape, dtype)


def call(name, kernel, outs, out_specs, ins, in_specs, scratch=(), after=(), flops=0, mib=16):
    late = len(after)

    def body(*refs):
        kernel(*refs[: len(ins)], *refs[len(ins) + late :])

    moved = sum(x.size * x.dtype.itemsize for x in (*ins, *outs))
    return pl.pallas_call(
        body,
        out_shape=list(outs),
        in_specs=list(in_specs) + [ANY] * late,
        out_specs=list(out_specs),
        scratch_shapes=list(scratch),
        compiler_params=pltpu.CompilerParams(vmem_limit_bytes=mib * 2**20),
        cost_estimate=pl.CostEstimate(flops=int(flops), bytes_accessed=int(moved), transcendentals=0),
        name=name,
    )(*ins, *after)


def placement(ids, here, members, slot, total):
    count = ids.shape[1]
    lanes = lax.broadcasted_iota(jnp.int32, (max(members, 8), count), 0)
    chosen = (lanes == ids).astype(F32)
    before = lax.broadcasted_iota(jnp.int32, (count, count), 0) < lax.broadcasted_iota(
        jnp.int32, (count, count), 1
    )
    ranks = mm(chosen.astype(BF16), before.astype(F32).astype(BF16))
    rank = jnp.sum(chosen * ranks, axis=0, keepdims=True).astype(jnp.int32)
    target = (ids ^ here) * slot + rank
    return lax.broadcasted_iota(jnp.int32, (total, count), 0) == target


def dispatch(ids, here, data, gates, members, slot, after=()):
    total, width, count = members * slot, data.shape[1], data.shape[0]
    gated = gates is not None
    small = [ids] + ([gates] if gated else [])

    def kernel(here_ref, *refs):
        sources = refs[: len(small) + 1]
        out_refs = refs[len(small) + 1 :][:members]
        held, sems = refs[len(small) + 1 + members : -1], refs[-1]
        copies = [
            pltpu.make_async_copy(s, h, sems.at[i]) for i, (s, h) in enumerate(zip(sources, held))
        ]
        for copy in copies:
            copy.start()
        for copy in copies[:-1]:
            copy.wait()
        mask = placement(held[0][...], here_ref[0], members, slot, total)
        value = held[1][...].astype(F32) if gated else 1.0
        pick = jnp.where(mask, value, 0.0).astype(BF16)
        copies[-1].wait()
        rows = mm(pick, held[-1][...]).astype(BF16)
        for m, ref in enumerate(out_refs):
            ref[...] = rows[m * slot : (m + 1) * slot]

    ins = [*small, data]
    return call(
        "dispatch",
        kernel,
        [spec((slot, width))] * members,
        [VMEM] * members,
        [here, *ins],
        [SMEM] + [ANY] * len(ins),
        [pltpu.VMEM(x.shape, x.dtype) for x in ins] + [pltpu.SemaphoreType.DMA((len(ins),))],
        after,
        2 * total * count * width,
    )


def collect(ids, here, rows, gates, members, slot, after=()):
    total, width, count = members * slot, rows[0].shape[1], ids.shape[1]
    gated = gates is not None
    small = [ids] + ([gates] if gated else [])

    def kernel(here_ref, *refs):
        row_refs = refs[len(small) : len(small) + members]
        out_ref, joined = refs[-2], refs[-1]
        for m, ref in enumerate(row_refs):
            joined[m * slot : (m + 1) * slot, :] = ref[...]
        mask = placement(refs[0][...], here_ref[0], members, slot, total)
        value = refs[1][...].astype(F32) if gated else 1.0
        pick = jnp.where(mask, value, 0.0).astype(BF16)
        out_ref[...] = mm(pick, joined[...], TN).astype(BF16)

    return call(
        "collect",
        kernel,
        [spec((count, width))],
        [VMEM],
        [here, *small, *rows],
        [SMEM] + [VMEM] * (len(small) + members),
        [pltpu.VMEM((total, width), BF16)],
        after,
        2 * count * total * width,
    )[0]


def load(arrays, after=()):
    def kernel(*refs):
        n = len(arrays)
        copies = [
            pltpu.make_async_copy(refs[i], refs[n + i], refs[-1].at[i]) for i in range(n)
        ]
        for copy in copies:
            copy.start()
        for copy in copies:
            copy.wait()

    return call(
        "load",
        kernel,
        [spec(x.shape, x.dtype) for x in arrays],
        [VMEM] * len(arrays),
        arrays,
        [ANY] * len(arrays),
        [pltpu.SemaphoreType.DMA((len(arrays),))],
        after,
    )


def block_of(ref, index, unit, axis):
    at = pl.ds(pl.multiple_of(index * unit, unit), unit)
    return ref[at, :] if axis == 0 else ref[:, at]


def away_terms(ids, rows, weights, unit, down, after=()):
    members, (slot, width) = len(rows), rows[0].shape
    total, n, blocks = members * slot, len(weights), ids.shape[0]

    def kernel(ids_ref, *refs):
        row_refs, w_refs = refs[:members], refs[members : members + n]
        out_ref, joined = refs[-2:]
        for m, ref in enumerate(row_refs):
            joined[m * slot : (m + 1) * slot, :] = ref[...]
        x = joined[...]
        for j in range(blocks):
            for i, w_ref in enumerate(w_refs):
                w = block_of(w_ref, ids_ref[j], unit, 0 if down else 1)
                out_ref[j, i] = mm(x, w, NT if down else NN).astype(BF16)

    return call(
        "away_terms",
        kernel,
        [spec((blocks, n, total, unit)), spec((total, width))],
        [VMEM] * 2,
        [ids, *rows, *weights],
        [SMEM] + [VMEM] * (members + n),
        (),
        after,
        2 * n * blocks * total * width * unit,
    )


def kept_terms(ids, joined, weights, arrived, unit, down, after=()):
    (total, width), n, blocks = joined.shape, len(weights), ids.shape[0]
    first = blocks // 2

    def kernel(ids_ref, x_ref, *refs):
        w_refs, (got, send, keep) = refs[:n], refs[n:]
        x = x_ref[...]
        for j in (*range(first, blocks), *range(first)):
            for i, w_ref in enumerate(w_refs):
                w = block_of(w_ref, ids_ref[j], unit, 0 if down else 1)
                term = mm(x, w, NT if down else NN) + got[j, i].astype(F32)
                if j >= first:
                    send[j - first, i] = term.astype(BF16)
                else:
                    keep[j, i] = term

    return call(
        "kept_terms",
        kernel,
        [spec((blocks - first, n, total, unit)), spec((first, n, total, unit), F32)],
        [VMEM] * 2,
        [ids, joined, *weights, arrived],
        [SMEM] + [VMEM] * (2 + n),
        (),
        after,
        2 * n * blocks * total * width * unit,
    )


def unit_rows(pieces, weights, unit, down, before=None, split=None, after=()):
    ids = [p[0] for p in pieces]
    units = [p[1] for p in pieces]
    n, total = units[0].shape[1], units[0].shape[2]
    width = weights[0].shape[1] if down else weights[0].shape[0]
    blocks = sum(u.shape[0] for u in units)
    started = [] if before is None else [before]
    k = len(pieces)

    def kernel(*refs):
        id_refs, u_refs, w_refs = refs[:k], refs[k : 2 * k], refs[2 * k : 2 * k + n]
        acc = refs[-1]
        start_refs = refs[2 * k + n : 2 * k + n + len(started)]
        out_refs = refs[2 * k + n + len(started) : -1]
        acc[...] = start_refs[0][...] if started else jnp.zeros_like(acc)
        for id_ref, u_ref in zip(id_refs, u_refs):
            for j in range(u_ref.shape[0]):
                term = None
                for i, w_ref in enumerate(w_refs):
                    w = block_of(w_ref, id_ref[j], unit, 0 if down else 1)
                    more = mm(u_ref[j, i], w, NN if down else NT)
                    term = more if term is None else term + more
                acc[...] += term
        if split is None:
            out_refs[0][...] = acc[...]
        else:
            for m, ref in enumerate(out_refs):
                ref[...] = acc[m * split : (m + 1) * split, :].astype(BF16)

    if split is None:
        outs = [spec((total, width), F32)]
    else:
        outs = [spec((split, width))] * (total // split)
    return call(
        "unit_rows",
        kernel,
        outs,
        [VMEM] * len(outs),
        [*ids, *units, *weights, *started],
        [SMEM] * k + [VMEM] * (k + n + len(started)),
        [pltpu.VMEM((total, width), F32)],
        after,
        2 * n * blocks * total * width * unit,
    )


def weight_grads(pieces, joined, unit, down, after=()):
    (total, width), k = joined.shape, len(pieces)
    ids = [p[0] for p in pieces]
    parts = len(pieces[0][1])
    units = [u for p in pieces for u in p[1]]
    n = units[0].shape[1]
    blocks = sum(p[1][0].shape[0] for p in pieces)
    shape = (1, blocks * unit, width) if down else (1, width, blocks * unit)

    def kernel(*refs):
        id_refs, u_refs, x_ref = refs[:k], refs[k : k + k * parts], refs[k + k * parts]
        out_refs = refs[k + k * parts + 1 :][:n]
        turned, rows, held, sems = refs[-4:]
        if not down:
            turned[...] = x_ref[...].T
        waits, step = [None, None], 0
        for p in range(k):
            for j in range(pieces[p][1][0].shape[0]):
                at = pl.ds(pl.multiple_of(id_refs[p][j] * unit, unit), unit)
                for i in range(n):
                    slot = step % 2
                    step += 1
                    if parts == 1:
                        u = u_refs[p][j, i]
                    else:
                        top = 0
                        for ref in u_refs[p * parts : (p + 1) * parts]:
                            rows[top : top + ref.shape[2], :] = ref[j, i]
                            top += ref.shape[2]
                        u = rows[...]
                    if waits[slot] is not None:
                        waits[slot].wait()
                    if down:
                        held[slot] = mm(u, x_ref[...], TN).astype(BF16)
                        target = out_refs[i].at[0, at, :]
                    else:
                        held[slot] = mm(turned[...], u).astype(BF16)
                        target = out_refs[i].at[0, :, at]
                    waits[slot] = pltpu.make_async_copy(held.at[slot], target, sems.at[slot])
                    waits[slot].start()
        for wait in waits:
            wait.wait()

    return call(
        "weight_grads",
        kernel,
        [spec(shape)] * n,
        [ANY] * n,
        [*ids, *units, joined],
        [SMEM] * k + [VMEM] * (k * parts + 1),
        [
            pltpu.VMEM((width, total), BF16),
            pltpu.VMEM((total, unit), BF16),
            pltpu.VMEM((2, unit, width) if down else (2, width, unit), BF16),
            pltpu.SemaphoreType.DMA((2,)),
        ],
        after,
        2 * n * blocks * total * width * unit,
    )


def hypercube(tokens, gate_weights, expert_ids, w_gate, w_up, w_down, grad_out):
    members = lax.axis_size("expert")
    parts = lax.axis_size("tensor")
    bits = (parts // 2).bit_length() - 1
    count = tokens.shape[0]
    slot = 3 * count // (2 * members)
    unit = w_gate.shape[2] // parts
    half = parts // 2

    here = lax.axis_index("expert").reshape(1)
    ids = expert_ids.reshape(1, count)
    gates = gate_weights.reshape(1, count)

    t = lax.axis_index("tensor")
    core, chip = t & 1, t >> 1
    orders = (tuple(range(bits)), tuple(reversed(range(bits))))

    def pairs(step):
        return [(d, d ^ (2 << orders[d % 2][step])) for d in range(parts)]

    def step_swap(x, step):
        return lax.ppermute(x, "tensor", pairs(step))

    def core_swap(x):
        return lax.ppermute(x, "tensor", [(d, d ^ 1) for d in range(parts)])

    def block_ids(c):
        rel = jnp.arange(half, dtype=jnp.int32)
        place = [jnp.zeros_like(rel), jnp.zeros_like(rel)]
        for k in range(2):
            for step in range(bits):
                bit = (chip >> orders[k][step]) & 1
                flip = (rel >> (bits - 1 - step)) & 1
                place[k] = place[k] * 2 + (bit ^ flip)
        return half * c + jnp.where(c == 0, place[0], place[1])

    mine, other = block_ids(core), block_ids(1 - core)

    def expert_swap(rows, skipped=1):
        return [
            lax.ppermute(rows[m - skipped], "expert", [(d, d ^ m) for d in range(members)])
            for m in range(1, members)
        ]

    def halve(send, keep):
        size = send.shape[0]
        for step in range(bits):
            got = step_swap(send, step)
            total = keep + got.astype(F32)
            size //= 2
            if step < bits - 1:
                send, keep = total[size:].astype(BF16), total[:size]
        return total[0]

    def gather_units(x):
        firsts = []
        for step in reversed(range(bits)):
            got = step_swap(x, step)
            firsts.append(got)
            x = jnp.concatenate([x, got], axis=0)
        return x, core_swap(x), firsts[0]

    def later(x, *others):
        return lax.optimization_barrier((x, *others))[0]

    x_slots = dispatch(ids, here, tokens, None, members, slot)
    x_rows = [x_slots[0]] + expert_swap(x_slots, 0)
    weight_gate, weight_up = load((w_gate[0], w_up[0]), (x_slots[1],))
    dy_slots = dispatch(ids, here, grad_out, gates, members, slot, (weight_gate,))
    dy_rows = [dy_slots[0]] + expert_swap(dy_slots, 0)

    away, x_all = away_terms(other, x_rows, (weight_gate, weight_up), unit, False, (dy_slots[1],))
    (weight_down,) = load((w_down[0],), (away,))
    send, keep = kept_terms(
        mine, x_all, (weight_gate, weight_up), core_swap(away), unit, False, (weight_down,)
    )
    away, dy_all = away_terms(other, dy_rows, (weight_down,), unit, True, (send,))
    gate, up = halve(send, keep)
    send, keep = kept_terms(mine, dy_all, (weight_down,), core_swap(away), unit, True)
    (d_hidden,) = halve(send, keep)

    sigma = jax.nn.sigmoid(gate)
    active = gate * sigma
    hidden = (active * up).astype(BF16)
    d_gate = (d_hidden * up * sigma * (1.0 + gate * (1.0 - sigma))).astype(BF16)
    d_up = (d_hidden * active).astype(BF16)
    d_far = jnp.stack([d_gate[slot:], d_up[slot:]])[None]
    d_own = jnp.stack([d_gate[:slot], d_up[:slot]])[None]

    hidden_mine, hidden_other, _ = gather_units(hidden[None, None])
    far_mine, far_other, first = gather_units(d_far)
    own_mine, own_other, _ = gather_units(later(d_own, first))

    hidden_pieces = ((mine, hidden_mine), (other, hidden_other))
    out = unit_rows(hidden_pieces, (weight_down,), unit, True, split=slot)
    out_back = expert_swap(out, 0)
    (grad_w_down,) = weight_grads(
        [(i, (u,)) for i, u in hidden_pieces], dy_all, unit, True, (out[0],)
    )

    gate_up = (weight_gate, weight_up)
    (back,) = unit_rows(((mine, far_mine),), gate_up, unit, False, after=(grad_w_down,))
    far = unit_rows(((other, far_other),), gate_up, unit, False, back, slot)
    grad_back = expert_swap(far, 1)
    (own,) = unit_rows(
        ((mine, own_mine), (other, own_other)), gate_up, unit, False, None, slot, (far[0],)
    )
    grad_w_gate, grad_w_up = weight_grads(
        ((mine, (own_mine, far_mine)), (other, (own_other, far_other))), x_all, unit, False, (own,)
    )

    mixed = collect(ids, here, [out[0]] + out_back, gates, members, slot)
    grad_tokens = collect(ids, here, [own] + grad_back, None, members, slot)
    return (mixed, grad_tokens, grad_w_gate, grad_w_up, grad_w_down)


def power_of_two(n):
    return n & (n - 1) == 0


def solution(mesh):
    members, parts = mesh.shape["expert"], mesh.shape["tensor"]

    def local(*args):
        unit = args[3].shape[2] // parts
        slot = 3 * args[0].shape[0] // (2 * members)
        fits = power_of_two(members) and power_of_two(parts) and parts >= 4
        fits = fits and unit % 128 == 0 and slot % 16 == 0 and args[0].shape[1] % 128 == 0
        fits = fits and args[2].shape[1] == 1
        return (hypercube if fits else general)(*args)

    in_specs = (
        P("expert", "tensor"),
        P("expert", None),
        P("expert", None),
        P("expert", "tensor", None),
        P("expert", "tensor", None),
        P("expert", None, "tensor"),
        P("expert", "tensor"),
    )
    out_specs = (
        P("expert", "tensor"),
        P("expert", "tensor"),
        P("expert", "tensor", None),
        P("expert", "tensor", None),
        P("expert", None, "tensor"),
    )
    return jax.shard_map(local, mesh=mesh, in_specs=in_specs, out_specs=out_specs, check_vma=False)
```

```python
import functools

import jax
import jax.numpy as jnp
from jax import lax
from jax.experimental import pallas as pl
from jax.experimental.pallas import tpu as pltpu
from jax.sharding import PartitionSpec as P

F32 = jnp.float32
BF16 = jnp.bfloat16


def spread_units(function):
    return lax.psum_scatter(function(), "tensor", scatter_dimension=0, tiled=True)


def general(tokens, gate_weights, expert_ids, w_gate, w_up, w_down, grad_out):
    members = lax.axis_size("expert")
    tok_rows = tokens.shape[0]
    routes = expert_ids.shape[1]
    width = tokens.shape[1]
    slot = 3 * routes * tok_rows // (2 * members)
    total = members * slot
    flat_ids = expert_ids.reshape(-1)
    counted = (flat_ids[:, None] == jnp.arange(members, dtype=jnp.int32)[None, :]).astype(jnp.int32)
    ranks = jnp.cumsum(counted, axis=0) - 1
    position = jnp.sum(counted * ranks, axis=1)
    target = (flat_ids * slot + position).reshape(tok_rows, routes)
    matched = target[None, :, :] == jnp.arange(total, dtype=jnp.int32)[:, None, None]
    place = jnp.sum(matched.astype(F32), axis=2).astype(BF16)
    weighted = jnp.sum(jnp.where(matched, gate_weights.astype(F32)[None], 0.0), axis=2).astype(BF16)
    x_slots = jnp.dot(place, tokens, preferred_element_type=F32).astype(BF16)
    dy_slots = jnp.dot(weighted, grad_out, preferred_element_type=F32).astype(BF16)
    outgoing = jnp.stack(
        [x_slots.reshape(members, slot, width), dy_slots.reshape(members, slot, width)], axis=1
    )
    arrived = lax.all_to_all(outgoing, "expert", split_axis=0, concat_axis=0, tiled=True)
    x_rows = arrived[:, 0].reshape(total, width)
    dy_rows = arrived[:, 1].reshape(total, width)
    weight_gate, weight_up, weight_down = w_gate[0], w_up[0], w_down[0]
    dot = functools.partial(lax.dot_general, preferred_element_type=F32)

    def gate_terms():
        return jnp.concatenate(
            [dot(w, x_rows, (((0,), (1,)), ((), ()))) for w in (weight_gate, weight_up)], axis=1
        )

    summed = spread_units(gate_terms)
    gate_t, up_t = summed[:, :total], summed[:, total:]
    sigma = jax.nn.sigmoid(gate_t)
    active = gate_t * sigma
    hidden_t = (active * up_t).astype(BF16)
    hidden = lax.all_gather(hidden_t, "tensor", axis=0, tiled=True)
    out_rows = dot(hidden, weight_down, (((0,), (0,)), ((), ()))).astype(BF16)
    swap = functools.partial(
        lax.all_to_all, axis_name="expert", split_axis=0, concat_axis=0, tiled=True
    )
    out_back = swap(out_rows.reshape(members, slot, width))
    d_hidden = spread_units(lambda: dot(weight_down, dy_rows, (((1,), (1,)), ((), ()))))
    d_gate_t = (d_hidden * up_t * sigma * (1.0 + gate_t * (1.0 - sigma))).astype(BF16)
    d_up_t = (d_hidden * active).astype(BF16)
    d_gate = lax.all_gather(d_gate_t, "tensor", axis=0, tiled=True)
    d_up = lax.all_gather(d_up_t, "tensor", axis=0, tiled=True)
    back_rows = (
        dot(d_gate, weight_gate, (((0,), (1,)), ((), ())))
        + dot(d_up, weight_up, (((0,), (1,)), ((), ())))
    ).astype(BF16)
    grad_w_gate = dot(x_rows, d_gate, (((0,), (1,)), ((), ()))).astype(BF16)[None]
    grad_w_up = dot(x_rows, d_up, (((0,), (1,)), ((), ()))).astype(BF16)[None]
    grad_w_down = dot(hidden, dy_rows, (((1,), (0,)), ((), ()))).astype(BF16)[None]
    grad_back = swap(back_rows.reshape(members, slot, width))
    mixed = dot(weighted, out_back.reshape(total, width), (((0,), (0,)), ((), ()))).astype(BF16)
    grad_tokens = dot(place, grad_back.reshape(total, width), (((0,), (0,)), ((), ()))).astype(BF16)
    return (mixed, grad_tokens, grad_w_gate, grad_w_up, grad_w_down)


NT = (((1,), (1,)), ((), ()))
TN = (((0,), (0,)), ((), ()))
NN = (((1,), (0,)), ((), ()))
VMEM = pl.BlockSpec(memory_space=pltpu.VMEM)
SMEM = pl.BlockSpec(memory_space=pltpu.SMEM)
ANY = pl.BlockSpec(memory_space=pl.ANY)


def mm(a, b, dims=NN):
    return lax.dot_general(a, b, dims, preferred_element_type=F32)


def in_hbm(x):
    return pltpu.with_memory_space_constraint(x, pltpu.HBM)


def spec(shape, dtype=BF16):
    return jax.ShapeDtypeStruct(shape, dtype)


def call(kernel, outs, out_specs, ins, in_specs, scratch=(), after=(), flops=0, mib=16):
    late = len(after)

    def body(*refs):
        kernel(*refs[: len(ins)], *refs[len(ins) + late :])

    moved = sum(x.size * x.dtype.itemsize for x in (*ins, *outs))
    return pl.pallas_call(
        body,
        out_shape=list(outs),
        in_specs=list(in_specs) + [ANY] * late,
        out_specs=list(out_specs),
        scratch_shapes=list(scratch),
        compiler_params=pltpu.CompilerParams(vmem_limit_bytes=mib * 2**20),
        cost_estimate=pl.CostEstimate(flops=int(flops), bytes_accessed=int(moved), transcendentals=0),
    )(*ins, *after)


def placement(ids, here, members, slot, total):
    count = ids.shape[1]
    lanes = lax.broadcasted_iota(jnp.int32, (max(members, 8), count), 0)
    chosen = (lanes == ids).astype(F32)
    before = lax.broadcasted_iota(jnp.int32, (count, count), 0) < lax.broadcasted_iota(
        jnp.int32, (count, count), 1
    )
    ranks = mm(chosen.astype(BF16), before.astype(F32).astype(BF16))
    rank = jnp.sum(chosen * ranks, axis=0, keepdims=True).astype(jnp.int32)
    target = (ids ^ here) * slot + rank
    return lax.broadcasted_iota(jnp.int32, (total, count), 0) == target


def dispatch(ids, here, gates, tokens, cotangents, members, slot):
    (count, width), total = tokens.shape, members * slot
    ins = [ids, gates, tokens, cotangents]

    def kernel(here_ref, *refs):
        sources, out_refs = refs[:4], refs[4 : 4 + 2 * members]
        held, sems = refs[4 + 2 * members : -1], refs[-1]
        copies = [
            pltpu.make_async_copy(s, h, sems.at[i]) for i, (s, h) in enumerate(zip(sources, held))
        ]
        for copy in copies:
            copy.start()
        copies[0].wait()
        copies[1].wait()
        mask = placement(held[0][...], here_ref[0], members, slot, total)
        gate = held[1][...].astype(F32)
        for i, value in enumerate((1.0, gate)):
            pick = jnp.where(mask, value, 0.0).astype(BF16)
            copies[2 + i].wait()
            rows = mm(pick, held[2 + i][...]).astype(BF16)
            for m in range(members):
                out_refs[members * i + m][...] = rows[m * slot : (m + 1) * slot]

    out = call(
        kernel,
        [spec((slot, width))] * (2 * members),
        [VMEM] * (2 * members),
        [here, *map(in_hbm, ins)],
        [SMEM] + [ANY] * 4,
        [pltpu.VMEM(x.shape, x.dtype) for x in ins] + [pltpu.SemaphoreType.DMA((4,))],
        (),
        4 * total * count * width,
    )
    return out[:members], out[members:]


def collect(ids, here, rows, gates, members, slot, after=()):
    total, width, count = members * slot, rows[0].shape[1], ids.shape[1]
    gated = gates is not None
    small = [ids] + ([gates] if gated else [])

    def kernel(here_ref, *refs):
        row_refs = refs[len(small) : len(small) + members]
        out_ref, joined = refs[-2], refs[-1]
        for m, ref in enumerate(row_refs):
            joined[m * slot : (m + 1) * slot, :] = ref[...]
        mask = placement(refs[0][...], here_ref[0], members, slot, total)
        value = refs[1][...].astype(F32) if gated else 1.0
        pick = jnp.where(mask, value, 0.0).astype(BF16)
        out_ref[...] = mm(pick, joined[...], TN).astype(BF16)

    return call(
        kernel,
        [spec((count, width))],
        [VMEM],
        [here, *small, *rows],
        [SMEM] + [VMEM] * (len(small) + members),
        [pltpu.VMEM((total, width), BF16)],
        after,
        2 * count * total * width,
    )[0]


def load(arrays, after=()):
    def kernel(*refs):
        n = len(arrays)
        copies = [
            pltpu.make_async_copy(refs[i], refs[n + i], refs[-1].at[i]) for i in range(n)
        ]
        for copy in copies:
            copy.start()
        for copy in copies:
            copy.wait()

    return call(
        kernel,
        [spec(x.shape, x.dtype) for x in arrays],
        [VMEM] * len(arrays),
        [in_hbm(x) for x in arrays],
        [ANY] * len(arrays),
        [pltpu.SemaphoreType.DMA((len(arrays),))],
        after,
    )


def block_of(ref, index, unit, axis):
    at = pl.ds(pl.multiple_of(index * unit, unit), unit)
    return ref[at, :] if axis == 0 else ref[:, at]


def away_terms(ids, rows, weights, unit, down, after=()):
    members, (slot, width) = len(rows), rows[0].shape
    total, n, blocks = members * slot, len(weights), ids.shape[0]

    def kernel(ids_ref, *refs):
        row_refs, w_refs = refs[:members], refs[members : members + n]
        out_ref, joined = refs[-2:]
        for m, ref in enumerate(row_refs):
            joined[m * slot : (m + 1) * slot, :] = ref[...]
        x = joined[...]
        for j in range(blocks):
            for i, w_ref in enumerate(w_refs):
                w = block_of(w_ref, ids_ref[j], unit, 0 if down else 1)
                out_ref[j, i] = mm(x, w, NT if down else NN).astype(BF16)

    return call(
        kernel,
        [spec((blocks, n, total, unit)), spec((total, width))],
        [VMEM] * 2,
        [ids, *rows, *weights],
        [SMEM] + [VMEM] * (members + n),
        (),
        after,
        2 * n * blocks * total * width * unit,
    )


def kept_terms(ids, joined, weights, arrived, unit, down, after=()):
    (total, width), n, blocks = joined.shape, len(weights), ids.shape[0]
    first = blocks // 2

    def kernel(ids_ref, x_ref, *refs):
        w_refs, (got, send, keep) = refs[:n], refs[n:]
        x = x_ref[...]
        for j in (*range(first, blocks), *range(first)):
            for i, w_ref in enumerate(w_refs):
                w = block_of(w_ref, ids_ref[j], unit, 0 if down else 1)
                term = mm(x, w, NT if down else NN) + got[j, i].astype(F32)
                if j >= first:
                    send[j - first, i] = term.astype(BF16)
                else:
                    keep[j, i] = term

    return call(
        kernel,
        [spec((blocks - first, n, total, unit)), spec((first, n, total, unit), F32)],
        [VMEM] * 2,
        [ids, joined, *weights, arrived],
        [SMEM] + [VMEM] * (2 + n),
        (),
        after,
        2 * n * blocks * total * width * unit,
    )


def unit_rows(pieces, weights, unit, down, before=None, split=None, after=()):
    ids = [p[0] for p in pieces]
    units = [p[1] for p in pieces]
    n, total = units[0].shape[1], units[0].shape[2]
    width = weights[0].shape[1] if down else weights[0].shape[0]
    blocks = sum(u.shape[0] for u in units)
    started = [] if before is None else [before]
    k = len(pieces)

    def kernel(*refs):
        id_refs, u_refs, w_refs = refs[:k], refs[k : 2 * k], refs[2 * k : 2 * k + n]
        acc = refs[-1]
        start_refs = refs[2 * k + n : 2 * k + n + len(started)]
        out_refs = refs[2 * k + n + len(started) : -1]
        acc[...] = start_refs[0][...] if started else jnp.zeros_like(acc)
        for id_ref, u_ref in zip(id_refs, u_refs):
            for j in range(u_ref.shape[0]):
                term = None
                for i, w_ref in enumerate(w_refs):
                    w = block_of(w_ref, id_ref[j], unit, 0 if down else 1)
                    more = mm(u_ref[j, i], w, NN if down else NT)
                    term = more if term is None else term + more
                acc[...] += term
        if split is None:
            out_refs[0][...] = acc[...]
        else:
            for m, ref in enumerate(out_refs):
                ref[...] = acc[m * split : (m + 1) * split, :].astype(BF16)

    if split is None:
        outs = [spec((total, width), F32)]
    else:
        outs = [spec((split, width))] * (total // split)
    return call(
        kernel,
        outs,
        [VMEM] * len(outs),
        [*ids, *units, *weights, *started],
        [SMEM] * k + [VMEM] * (k + n + len(started)),
        [pltpu.VMEM((total, width), F32)],
        after,
        2 * n * blocks * total * width * unit,
    )


def weight_grads(pieces, joined, unit, down, after=()):
    (total, width), k = joined.shape, len(pieces)
    ids = [p[0] for p in pieces]
    parts = len(pieces[0][1])
    units = [u for p in pieces for u in p[1]]
    n = units[0].shape[1]
    blocks = sum(p[1][0].shape[0] for p in pieces)
    shape = (1, blocks * unit, width) if down else (1, width, blocks * unit)

    def kernel(*refs):
        id_refs, u_refs, x_ref = refs[:k], refs[k : k + k * parts], refs[k + k * parts]
        out_refs = refs[k + k * parts + 1 :][:n]
        turned, rows, held, sems = refs[-4:]
        if not down:
            turned[...] = x_ref[...].T
        waits = []
        for p in range(k):
            for j in range(pieces[p][1][0].shape[0]):
                at = pl.ds(pl.multiple_of(id_refs[p][j] * unit, unit), unit)
                for i in range(n):
                    slot = len(waits)
                    if parts == 1:
                        u = u_refs[p][j, i]
                    else:
                        top = 0
                        for ref in u_refs[p * parts : (p + 1) * parts]:
                            rows[top : top + ref.shape[2], :] = ref[j, i]
                            top += ref.shape[2]
                        u = rows[...]
                    if down:
                        held[slot] = mm(u, x_ref[...], TN).astype(BF16)
                        target = out_refs[i].at[0, at, :]
                    else:
                        held[slot] = mm(turned[...], u).astype(BF16)
                        target = out_refs[i].at[0, :, at]
                    waits.append(pltpu.make_async_copy(held.at[slot], target, sems.at[slot]))
                    waits[slot].start()
        for wait in waits:
            wait.wait()

    return call(
        kernel,
        [spec(shape)] * n,
        [ANY] * n,
        [*ids, *units, joined],
        [SMEM] * k + [VMEM] * (k * parts + 1),
        [
            pltpu.VMEM((width, total), BF16),
            pltpu.VMEM((total, unit), BF16),
            pltpu.VMEM((n * blocks, unit, width) if down else (n * blocks, width, unit), BF16),
            pltpu.SemaphoreType.DMA((n * blocks,)),
        ],
        after,
        2 * n * blocks * total * width * unit,
    )


def hypercube(tokens, gate_weights, expert_ids, w_gate, w_up, w_down, grad_out):
    members = lax.axis_size("expert")
    parts = lax.axis_size("tensor")
    bits = (parts // 2).bit_length() - 1
    count = tokens.shape[0]
    slot = 3 * count // (2 * members)
    unit = w_gate.shape[2] // parts
    half = parts // 2

    here = lax.axis_index("expert").reshape(1)
    ids = expert_ids.reshape(1, count)
    gates = gate_weights.reshape(1, count)

    t = lax.axis_index("tensor")
    core, chip = t & 1, t >> 1
    forward = tuple(range(bits))
    halving = (forward, forward[::-1])
    doubling = (forward[::-1], forward[::-1])

    def step_swap(x, orders, step):
        pairs = [(d, d ^ (2 << orders[d % 2][step])) for d in range(parts)]
        return lax.ppermute(x, "tensor", pairs)

    def core_swap(x):
        return lax.ppermute(x, "tensor", [(d, d ^ 1) for d in range(parts)])

    def block_ids(c, orders):
        rel = jnp.arange(half, dtype=jnp.int32)
        place = []
        for k in range(2):
            at = jnp.broadcast_to(chip, rel.shape)
            for step, bit in enumerate(orders[k]):
                at = at ^ (((rel >> (bits - 1 - step)) & 1) << bit)
            block = jnp.zeros_like(rel)
            for bit in halving[k]:
                block = block * 2 + ((at >> bit) & 1)
            place.append(block)
        return half * c + jnp.where(c == 0, place[0], place[1])

    here_ids, there_ids = block_ids(core, halving), block_ids(1 - core, halving)
    turned = tuple(order[::-1] for order in doubling)
    mine, other = block_ids(core, turned), block_ids(1 - core, turned)

    def expert_swap(rows, skipped=0):
        out = []
        for m in range(1, members):
            pairs = [(d, d ^ m) for d in range(members)]
            out.append(lax.ppermute(rows[m - skipped], "expert", pairs))
        return out

    def halve(send, keep):
        size = send.shape[0]
        for step in range(bits):
            got = step_swap(send, halving, step)
            total = keep + got.astype(F32)
            size //= 2
            if step < bits - 1:
                send, keep = total[size:].astype(BF16), total[:size]
        return total[0]

    def gather_units(x):
        for step in range(bits):
            got = step_swap(x, doubling, step)
            x = jnp.concatenate([x, got], axis=0)
        return x, core_swap(x)

    x_slots, dy_slots = dispatch(ids, here, gates, tokens, grad_out, members, slot)
    x_rows = [x_slots[0]] + expert_swap(x_slots)
    weight_gate, weight_up, weight_down = load(
        (w_gate[0], w_up[0], w_down[0]), (x_slots[1], here_ids, there_ids, mine, other)
    )
    gate_up = (weight_gate, weight_up)
    dy_rows = [dy_slots[0]] + expert_swap(dy_slots)

    away, x_all = away_terms(there_ids, x_rows, gate_up, unit, False)
    send, keep = kept_terms(here_ids, x_all, gate_up, core_swap(away), unit, False)
    away, dy_all = away_terms(there_ids, dy_rows, (weight_down,), unit, True, (send,))
    gate, up = halve(send, keep)
    send, keep = kept_terms(here_ids, dy_all, (weight_down,), core_swap(away), unit, True)
    (d_hidden,) = halve(send, keep)

    sigma = jax.nn.sigmoid(gate)
    active = gate * sigma
    hidden = (active * up).astype(BF16)
    d_gate = (d_hidden * up * sigma * (1.0 + gate * (1.0 - sigma))).astype(BF16)
    d_up = (d_hidden * active).astype(BF16)
    d_far = jnp.stack([d_gate[slot:], d_up[slot:]])[None]
    d_own = jnp.stack([d_gate[:slot], d_up[:slot]])[None]

    hidden_mine, hidden_other = gather_units(hidden[None, None])
    far_mine, far_other = gather_units(d_far)
    own_mine, own_other = gather_units(d_own)

    hidden_pieces = ((mine, hidden_mine), (other, hidden_other))
    out = unit_rows(hidden_pieces, (weight_down,), unit, True, split=slot)
    out_back = expert_swap(out)
    (grad_w_down,) = weight_grads(
        [(i, (u,)) for i, u in hidden_pieces], dy_all, unit, True, (out[0],)
    )

    (back,) = unit_rows(((mine, far_mine),), gate_up, unit, False, after=(out[0],))
    far = unit_rows(((other, far_other),), gate_up, unit, False, back, slot)
    grad_back = expert_swap(far, 1)
    mixed = collect(ids, here, [out[0]] + out_back, gates, members, slot, (in_hbm(grad_w_down),))
    (own,) = unit_rows(
        ((mine, own_mine), (other, own_other)), gate_up, unit, False, None, slot, (mixed,)
    )
    grad_w_gate, grad_w_up = weight_grads(
        ((mine, (own_mine, far_mine)), (other, (own_other, far_other))), x_all, unit, False, (own,)
    )

    grad_tokens = collect(ids, here, [own] + grad_back, None, members, slot)
    return (mixed, grad_tokens, grad_w_gate, grad_w_up, grad_w_down)


def power_of_two(n):
    return n & (n - 1) == 0


def solution(mesh):
    members, parts = mesh.shape["expert"], mesh.shape["tensor"]

    def local(*args):
        unit = args[3].shape[2] // parts
        slot = 3 * args[0].shape[0] // (2 * members)
        fits = power_of_two(members) and power_of_two(parts) and parts >= 4
        fits = fits and unit % 128 == 0 and slot % 16 == 0 and args[0].shape[1] % 128 == 0
        fits = fits and args[2].shape[1] == 1
        return (hypercube if fits else general)(*args)

    in_specs = (
        P("expert", "tensor"),
        P("expert", None),
        P("expert", None),
        P("expert", "tensor", None),
        P("expert", "tensor", None),
        P("expert", None, "tensor"),
        P("expert", "tensor"),
    )
    out_specs = (
        P("expert", "tensor"),
        P("expert", "tensor"),
        P("expert", "tensor", None),
        P("expert", "tensor", None),
        P("expert", None, "tensor"),
    )
    return jax.shard_map(local, mesh=mesh, in_specs=in_specs, out_specs=out_specs, check_vma=False)
```

```python
import functools

import jax
import jax.numpy as jnp
from jax import lax
from jax.experimental import pallas as pl
from jax.experimental.pallas import tpu as pltpu
from jax.sharding import PartitionSpec as P


F32 = jnp.float32
BF16 = jnp.bfloat16


def spread_units(function):
    return lax.psum_scatter(function(), "tensor", scatter_dimension=0, tiled=True)


def general(tokens, gate_weights, expert_ids, w_gate, w_up, w_down, grad_out):
    members = lax.axis_size("expert")
    tok_rows = tokens.shape[0]
    routes = expert_ids.shape[1]
    width = tokens.shape[1]
    slot = 3 * routes * tok_rows // (2 * members)
    total = members * slot
    flat_ids = expert_ids.reshape(-1)
    counted = (flat_ids[:, None] == jnp.arange(members, dtype=jnp.int32)[None, :]).astype(jnp.int32)
    ranks = jnp.cumsum(counted, axis=0) - 1
    position = jnp.sum(counted * ranks, axis=1)
    target = (flat_ids * slot + position).reshape(tok_rows, routes)
    matched = target[None, :, :] == jnp.arange(total, dtype=jnp.int32)[:, None, None]
    place = jnp.sum(matched.astype(F32), axis=2).astype(BF16)
    weighted = jnp.sum(jnp.where(matched, gate_weights.astype(F32)[None], 0.0), axis=2).astype(BF16)
    x_slots = jnp.dot(place, tokens, preferred_element_type=F32).astype(BF16)
    dy_slots = jnp.dot(weighted, grad_out, preferred_element_type=F32).astype(BF16)
    outgoing = jnp.stack(
        [x_slots.reshape(members, slot, width), dy_slots.reshape(members, slot, width)], axis=1
    )
    arrived = lax.all_to_all(outgoing, "expert", split_axis=0, concat_axis=0, tiled=True)
    x_rows = arrived[:, 0].reshape(total, width)
    dy_rows = arrived[:, 1].reshape(total, width)
    weight_gate, weight_up, weight_down = w_gate[0], w_up[0], w_down[0]
    dot = functools.partial(lax.dot_general, preferred_element_type=F32)

    def gate_terms():
        return jnp.concatenate(
            [dot(w, x_rows, (((0,), (1,)), ((), ()))) for w in (weight_gate, weight_up)], axis=1
        )

    summed = spread_units(gate_terms)
    gate_t, up_t = summed[:, :total], summed[:, total:]
    sigma = jax.nn.sigmoid(gate_t)
    active = gate_t * sigma
    hidden_t = (active * up_t).astype(BF16)
    hidden = lax.all_gather(hidden_t, "tensor", axis=0, tiled=True)
    out_rows = dot(hidden, weight_down, (((0,), (0,)), ((), ()))).astype(BF16)
    swap = functools.partial(
        lax.all_to_all, axis_name="expert", split_axis=0, concat_axis=0, tiled=True
    )
    out_back = swap(out_rows.reshape(members, slot, width))
    d_hidden = spread_units(lambda: dot(weight_down, dy_rows, (((1,), (1,)), ((), ()))))
    d_gate_t = (d_hidden * up_t * sigma * (1.0 + gate_t * (1.0 - sigma))).astype(BF16)
    d_up_t = (d_hidden * active).astype(BF16)
    d_gate = lax.all_gather(d_gate_t, "tensor", axis=0, tiled=True)
    d_up = lax.all_gather(d_up_t, "tensor", axis=0, tiled=True)
    back_rows = (
        dot(d_gate, weight_gate, (((0,), (1,)), ((), ())))
        + dot(d_up, weight_up, (((0,), (1,)), ((), ())))
    ).astype(BF16)
    grad_w_gate = dot(x_rows, d_gate, (((0,), (1,)), ((), ()))).astype(BF16)[None]
    grad_w_up = dot(x_rows, d_up, (((0,), (1,)), ((), ()))).astype(BF16)[None]
    grad_w_down = dot(hidden, dy_rows, (((1,), (0,)), ((), ()))).astype(BF16)[None]
    grad_back = swap(back_rows.reshape(members, slot, width))
    mixed = dot(weighted, out_back.reshape(total, width), (((0,), (0,)), ((), ()))).astype(BF16)
    grad_tokens = dot(place, grad_back.reshape(total, width), (((0,), (0,)), ((), ()))).astype(BF16)
    return (mixed, grad_tokens, grad_w_gate, grad_w_up, grad_w_down)


NT = (((1,), (1,)), ((), ()))
TN = (((0,), (0,)), ((), ()))
NN = (((1,), (0,)), ((), ()))
VMEM = pl.BlockSpec(memory_space=pltpu.VMEM)
ANY = pl.BlockSpec(memory_space=pl.ANY)


def mm(a, b, dims=NN):
    return lax.dot_general(a, b, dims, preferred_element_type=F32)


def in_hbm(x):
    return pltpu.with_memory_space_constraint(x, pltpu.HBM)


def spec(shape, dtype=BF16):
    return jax.ShapeDtypeStruct(shape, dtype)


def call(kernel, outs, out_specs, ins, in_specs, scratch=(), after=(), flops=0, mib=16):
    late = len(after)

    def body(*refs):
        kernel(*refs[: len(ins)], *refs[len(ins) + late :])

    moved = sum(x.size * x.dtype.itemsize for x in (*ins, *outs))
    return pl.pallas_call(
        body,
        out_shape=list(outs),
        in_specs=list(in_specs) + [ANY] * late,
        out_specs=list(out_specs),
        scratch_shapes=list(scratch),
        compiler_params=pltpu.CompilerParams(vmem_limit_bytes=mib * 2**20),
        cost_estimate=pl.CostEstimate(flops=int(flops), bytes_accessed=int(moved), transcendentals=0),
    )(*ins, *after)


def placement(ids, members, slot, total):
    count = ids.shape[1]
    lanes = lax.broadcasted_iota(jnp.int32, (max(members, 8), count), 0)
    chosen = (lanes == ids).astype(F32)
    before = lax.broadcasted_iota(jnp.int32, (count, count), 0) < lax.broadcasted_iota(
        jnp.int32, (count, count), 1
    )
    ranks = mm(chosen.astype(BF16), before.astype(F32).astype(BF16))
    rank = jnp.sum(chosen * ranks, axis=0, keepdims=True).astype(jnp.int32)
    target = (ids ^ lax.axis_index("expert")) * slot + rank
    return lax.broadcasted_iota(jnp.int32, (total, count), 0) == target


def dispatch(ids, gates, tokens, cotangents, members, slot):
    (count, width), total = tokens.shape, members * slot
    ins = [ids, gates, tokens, cotangents]

    def kernel(*refs):
        sources, out_refs = refs[:4], refs[4 : 4 + 2 * members]
        held, sems = refs[4 + 2 * members : -1], refs[-1]
        copies = [
            pltpu.make_async_copy(s, h, sems.at[i]) for i, (s, h) in enumerate(zip(sources, held))
        ]
        for copy in copies:
            copy.start()
        copies[0].wait()
        copies[1].wait()
        mask = placement(held[0][...], members, slot, total)
        gate = held[1][...].astype(F32)
        for i, value in enumerate((1.0, gate)):
            pick = jnp.where(mask, value, 0.0).astype(BF16)
            copies[2 + i].wait()
            rows = mm(pick, held[2 + i][...]).astype(BF16)
            for m in range(members):
                out_refs[members * i + m][...] = rows[m * slot : (m + 1) * slot]

    out = call(
        kernel,
        [spec((slot, width))] * (2 * members),
        [VMEM] * (2 * members),
        [*map(in_hbm, ins)],
        [ANY] * 4,
        [pltpu.VMEM(x.shape, x.dtype) for x in ins] + [pltpu.SemaphoreType.DMA((4,))],
        (),
        4 * total * count * width,
    )
    return out[:members], out[members:]


def plan(ids, gates, members, slot, after=()):
    count, total = ids.shape[1], members * slot

    def kernel(ids_ref, gates_ref, plain, gated):
        mask = placement(ids_ref[...], members, slot, total)
        plain[...] = jnp.where(mask, 1.0, 0.0).T.astype(BF16)
        gated[...] = jnp.where(mask, gates_ref[...].astype(F32), 0.0).T.astype(BF16)

    return call(
        kernel, [spec((count, total))] * 2, [VMEM] * 2, [ids, gates], [VMEM, VMEM], (), after
    )


def collect(picks, rows, after=()):
    (count, total), (slot, width) = picks.shape, rows[0].shape

    def kernel(picks_ref, *refs):
        row_refs, out_ref, joined = refs[:-2], refs[-2], refs[-1]
        for m, ref in enumerate(row_refs):
            joined[m * slot : (m + 1) * slot, :] = ref[...]
        out_ref[...] = mm(picks_ref[...], joined[...]).astype(BF16)

    return call(
        kernel,
        [spec((count, width))],
        [VMEM],
        [picks, *rows],
        [VMEM] * (1 + len(rows)),
        [pltpu.VMEM((total, width), BF16)],
        after,
        2 * count * total * width,
    )[0]


def load(arrays, after=()):
    def kernel(*refs):
        n = len(arrays)
        copies = [
            pltpu.make_async_copy(refs[i], refs[n + i], refs[-1].at[i]) for i in range(n)
        ]
        for copy in copies:
            copy.start()
        for copy in copies:
            copy.wait()

    return call(
        kernel,
        [spec(x.shape, x.dtype) for x in arrays],
        [VMEM] * len(arrays),
        [in_hbm(x) for x in arrays],
        [ANY] * len(arrays),
        [pltpu.SemaphoreType.DMA((len(arrays),))],
        after,
    )


def block_of(ref, index, unit, axis):
    at = pl.ds(pl.multiple_of(index * unit, unit), unit)
    return ref[at, :] if axis == 0 else ref[:, at]


def away_terms(block, rows, weights, blocks, unit, down, after=()):
    members, (slot, width) = len(rows), rows[0].shape
    total, n = members * slot, len(weights)

    def kernel(*refs):
        row_refs, w_refs = refs[:members], refs[members : members + n]
        out_ref, joined = refs[-2:]
        for m, ref in enumerate(row_refs):
            joined[m * slot : (m + 1) * slot, :] = ref[...]
        x = joined[...]
        for j in range(blocks):
            for i, w_ref in enumerate(w_refs):
                w = block_of(w_ref, block(j), unit, 0 if down else 1)
                out_ref[j, i] = mm(x, w, NT if down else NN).astype(BF16)

    return call(
        kernel,
        [spec((blocks, n, total, unit)), spec((total, width))],
        [VMEM] * 2,
        [*rows, *weights],
        [VMEM] * (members + n),
        (),
        after,
        2 * n * blocks * total * width * unit,
    )


def kept_terms(block, joined, weights, arrived, unit, down, after=()):
    (total, width), n, blocks = joined.shape, len(weights), arrived.shape[0]
    first = blocks // 2

    def kernel(x_ref, *refs):
        w_refs, (got, send, keep) = refs[:n], refs[n:]
        x = x_ref[...]
        for j in (*range(first, blocks), *range(first)):
            for i, w_ref in enumerate(w_refs):
                w = block_of(w_ref, block(j), unit, 0 if down else 1)
                term = mm(x, w, NT if down else NN) + got[j, i].astype(F32)
                if j >= first:
                    send[j - first, i] = term.astype(BF16)
                else:
                    keep[j, i] = term

    return call(
        kernel,
        [spec((blocks - first, n, total, unit)), spec((first, n, total, unit), F32)],
        [VMEM] * 2,
        [joined, *weights, arrived],
        [VMEM] * (2 + n),
        (),
        after,
        2 * n * blocks * total * width * unit,
    )


def unit_rows(terms, unit, down, before=None, split=None, after=()):
    weights = [w for w, _ in terms]
    pieces = [(i, *piece) for i, (_, group) in enumerate(terms) for piece in group]
    units = [u for _, _, _, u in pieces]
    total = units[0].shape[2]
    width = weights[0].shape[1] if down else weights[0].shape[0]
    started = [] if before is None else [before]
    k, n = len(pieces), len(weights)

    def kernel(*refs):
        u_refs, w_refs, rest = refs[:k], refs[k : k + n], refs[k + n :]
        out_refs = rest[len(started) :]
        held, blocks = [], []
        for (i, block, first, _), u_ref in zip(pieces, u_refs):
            for j in range(u_ref.shape[0]):
                held.append(u_ref[j, 0])
                blocks.append(block_of(w_refs[i], block(first + j), unit, 0 if down else 1))
        acc = mm(
            jnp.concatenate(held, axis=1),
            jnp.concatenate(blocks, axis=0 if down else 1),
            NN if down else NT,
        )
        if started:
            acc = acc + rest[0][...]
        if split is None:
            out_refs[0][...] = acc
        else:
            for m, ref in enumerate(out_refs):
                ref[...] = acc[m * split : (m + 1) * split, :].astype(BF16)

    if split is None:
        outs = [spec((total, width), F32)]
    else:
        outs = [spec((split, width))] * (total // split)
    return call(
        kernel,
        outs,
        [VMEM] * len(outs),
        [*units, *weights, *started],
        [VMEM] * (k + n + len(started)),
        (),
        after,
        2 * sum(u.shape[0] for u in units) * total * width * unit,
    )


def weight_grads(groups, joined, unit, down, after=()):
    total, width = joined.shape
    pieces = [(i, *piece) for i, group in enumerate(groups) for piece in group]
    units = [u for _, _, _, u in pieces]
    k, n = len(pieces), len(groups)
    steps = sum(u.shape[0] for u in units)
    blocks = steps // n
    shape = (1, blocks * unit, width) if down else (1, width, blocks * unit)

    def kernel(*refs):
        u_refs, x_ref, out_refs = refs[:k], refs[k], refs[k + 1 :][:n]
        turned, held, sems = refs[-3:]
        if not down:
            turned[...] = x_ref[...].T
        waits = []
        for (i, block, first, _), u_ref in zip(pieces, u_refs):
            for j in range(u_ref.shape[0]):
                at = pl.ds(pl.multiple_of(block(first + j) * unit, unit), unit)
                slot = len(waits)
                if down:
                    held[slot] = mm(u_ref[j, 0], x_ref[...], TN).astype(BF16)
                    target = out_refs[i].at[0, at, :]
                else:
                    held[slot] = mm(turned[...], u_ref[j, 0]).astype(BF16)
                    target = out_refs[i].at[0, :, at]
                waits.append(pltpu.make_async_copy(held.at[slot], target, sems.at[slot]))
                waits[slot].start()
        for wait in waits:
            wait.wait()

    return call(
        kernel,
        [spec(shape)] * n,
        [ANY] * n,
        [*units, joined],
        [VMEM] * (k + 1),
        [
            pltpu.VMEM((8, 128) if down else (width, total), BF16),
            pltpu.VMEM((steps, unit, width) if down else (steps, width, unit), BF16),
            pltpu.SemaphoreType.DMA((steps,)),
        ],
        after,
        2 * steps * total * width * unit,
    )


def hypercube(tokens, gate_weights, expert_ids, w_gate, w_up, w_down, grad_out):
    members = lax.axis_size("expert")
    parts = lax.axis_size("tensor")
    bits = (parts // 2).bit_length() - 1
    count = tokens.shape[0]
    slot = 3 * count // (2 * members)
    unit = w_gate.shape[2] // parts
    half = parts // 2

    ids = expert_ids.reshape(1, count)
    gates = gate_weights.reshape(1, count)

    forward = tuple(range(bits))
    halving = (forward, forward[::-1])
    doubling = (forward[::-1], forward[::-1])

    def step_swap(x, orders, step):
        pairs = [(d, d ^ (2 << orders[d % 2][step])) for d in range(parts)]
        return lax.ppermute(x, "tensor", pairs)

    def core_swap(x):
        return lax.ppermute(x, "tensor", [(d, d ^ 1) for d in range(parts)])

    def blocks_by(orders, other):
        def block(rel):
            t = lax.axis_index("tensor")
            core, chip = (t & 1) ^ other, t >> 1
            found = []
            for k in range(2):
                at = chip
                for step, bit in enumerate(orders[k]):
                    at = at ^ (((rel >> (bits - 1 - step)) & 1) << bit)
                index = jnp.int32(0)
                for bit in halving[k]:
                    index = index * 2 + ((at >> bit) & 1)
                found.append(index)
            return half * core + jnp.where(core == 0, found[0], found[1])

        return block

    here_ids, there_ids = blocks_by(halving, 0), blocks_by(halving, 1)
    turned = tuple(order[::-1] for order in doubling)
    mine, other = blocks_by(turned, 0), blocks_by(turned, 1)

    def expert_swap(rows, skipped=0):
        out = []
        for m in range(1, members):
            pairs = [(d, d ^ m) for d in range(members)]
            out.append(lax.ppermute(rows[m - skipped], "expert", pairs))
        return out

    def halve(send, keep):
        size = send.shape[0]
        for step in range(bits):
            got = step_swap(send, halving, step)
            total = keep + got.astype(F32)
            size //= 2
            if step < bits - 1:
                send, keep = total[size:].astype(BF16), total[:size]
        return total[0]

    def gather_units(x):
        for step in range(bits - 1):
            x = jnp.concatenate([x, step_swap(x, doubling, step)], axis=0)
        got = step_swap(x, doubling, bits - 1)
        size = x.shape[0]
        early = ((mine, 0, x), (other, 0, core_swap(x)))
        late = ((mine, size, got), (other, size, core_swap(got)))
        return early, late

    x_slots, dy_slots = dispatch(ids, gates, tokens, grad_out, members, slot)
    x_rows = [x_slots[0]] + expert_swap(x_slots)
    weight_gate, weight_up, weight_down = load(
        (w_gate[0], w_up[0], w_down[0]), (x_slots[1],)
    )
    plain, gated = plan(ids, gates, members, slot, (weight_gate,))
    gate_up = (weight_gate, weight_up)
    dy_rows = [dy_slots[0]] + expert_swap(dy_slots)

    away, x_all = away_terms(there_ids, x_rows, gate_up, half, unit, False, (plain,))
    send, keep = kept_terms(here_ids, x_all, gate_up, core_swap(away), unit, False)
    away, dy_all = away_terms(there_ids, dy_rows, (weight_down,), half, unit, True, (send,))
    gate, up = halve(send, keep)
    send, keep = kept_terms(here_ids, dy_all, (weight_down,), core_swap(away), unit, True)
    (d_hidden,) = halve(send, keep)

    hidden = (gate * jax.nn.sigmoid(gate) * up).astype(BF16)
    hidden, gate, up = lax.optimization_barrier((hidden, gate, up))
    sigma = jax.nn.sigmoid(gate)
    active = gate * sigma
    d_gate = (d_hidden * up * sigma * (1.0 + gate * (1.0 - sigma))).astype(BF16)
    d_up = (d_hidden * active).astype(BF16)

    hidden_early, hidden_late = gather_units(hidden[None, None])
    up_early, up_late = gather_units(d_up[None, None])
    gate_early, gate_late = gather_units(d_gate[None, None])
    hidden_all, up_all, gate_all = (
        hidden_early + hidden_late,
        up_early + up_late,
        gate_early + gate_late,
    )

    out = unit_rows(((weight_down, hidden_all),), unit, True, split=slot)
    out_back = expert_swap(out)
    (grad_w_down,) = weight_grads((hidden_all,), dy_all, unit, True, (out[0],))

    (part,) = unit_rows(
        ((weight_up, up_all), (weight_gate, gate_early)), unit, False, after=(in_hbm(grad_w_down),)
    )
    back = unit_rows(((weight_gate, gate_late),), unit, False, part, slot)
    grad_back = expert_swap(back)
    grad_w_gate, grad_w_up = weight_grads((gate_all, up_all), x_all, unit, False, (back[0],))
    mixed = collect(gated, [out[0]] + out_back, (in_hbm(grad_w_gate),))
    grad_tokens = collect(plain, [back[0]] + grad_back)
    return (mixed, grad_tokens, grad_w_gate, grad_w_up, grad_w_down)


def power_of_two(n):
    return n & (n - 1) == 0


def solution(mesh):
    members, parts = mesh.shape["expert"], mesh.shape["tensor"]

    def local(*args):
        unit = args[3].shape[2] // parts
        slot = 3 * args[0].shape[0] // (2 * members)
        fits = power_of_two(members) and power_of_two(parts) and parts >= 4
        fits = fits and unit % 128 == 0 and slot % 16 == 0 and args[0].shape[1] % 128 == 0
        fits = fits and args[2].shape[1] == 1
        return (hypercube if fits else general)(*args)

    in_specs = (
        P("expert", "tensor"),
        P("expert", None),
        P("expert", None),
        P("expert", "tensor", None),
        P("expert", "tensor", None),
        P("expert", None, "tensor"),
        P("expert", "tensor"),
    )
    out_specs = (
        P("expert", "tensor"),
        P("expert", "tensor"),
        P("expert", "tensor", None),
        P("expert", "tensor", None),
        P("expert", None, "tensor"),
    )
    return jax.shard_map(local, mesh=mesh, in_specs=in_specs, out_specs=out_specs, check_vma=False)
```

```python
import functools

import jax
import jax.numpy as jnp
from jax import lax
from jax.experimental import pallas as pl
from jax.experimental.pallas import tpu as pltpu
from jax.sharding import PartitionSpec as P


F32 = jnp.float32
BF16 = jnp.bfloat16


def spread_units(function):
    return lax.psum_scatter(function(), "tensor", scatter_dimension=0, tiled=True)


def general(tokens, gate_weights, expert_ids, w_gate, w_up, w_down, grad_out):
    members = lax.axis_size("expert")
    tok_rows = tokens.shape[0]
    routes = expert_ids.shape[1]
    width = tokens.shape[1]
    slot = 3 * routes * tok_rows // (2 * members)
    total = members * slot
    flat_ids = expert_ids.reshape(-1)
    counted = (flat_ids[:, None] == jnp.arange(members, dtype=jnp.int32)[None, :]).astype(jnp.int32)
    ranks = jnp.cumsum(counted, axis=0) - 1
    position = jnp.sum(counted * ranks, axis=1)
    target = (flat_ids * slot + position).reshape(tok_rows, routes)
    matched = target[None, :, :] == jnp.arange(total, dtype=jnp.int32)[:, None, None]
    place = jnp.sum(matched.astype(F32), axis=2).astype(BF16)
    weighted = jnp.sum(jnp.where(matched, gate_weights.astype(F32)[None], 0.0), axis=2).astype(BF16)
    x_slots = jnp.dot(place, tokens, preferred_element_type=F32).astype(BF16)
    dy_slots = jnp.dot(weighted, grad_out, preferred_element_type=F32).astype(BF16)
    outgoing = jnp.stack(
        [x_slots.reshape(members, slot, width), dy_slots.reshape(members, slot, width)], axis=1
    )
    arrived = lax.all_to_all(outgoing, "expert", split_axis=0, concat_axis=0, tiled=True)
    x_rows = arrived[:, 0].reshape(total, width)
    dy_rows = arrived[:, 1].reshape(total, width)
    weight_gate, weight_up, weight_down = w_gate[0], w_up[0], w_down[0]
    dot = functools.partial(lax.dot_general, preferred_element_type=F32)

    def gate_terms():
        return jnp.concatenate(
            [dot(w, x_rows, (((0,), (1,)), ((), ()))) for w in (weight_gate, weight_up)], axis=1
        )

    summed = spread_units(gate_terms)
    gate_t, up_t = summed[:, :total], summed[:, total:]
    sigma = jax.nn.sigmoid(gate_t)
    active = gate_t * sigma
    hidden_t = (active * up_t).astype(BF16)
    hidden = lax.all_gather(hidden_t, "tensor", axis=0, tiled=True)
    out_rows = dot(hidden, weight_down, (((0,), (0,)), ((), ()))).astype(BF16)
    swap = functools.partial(
        lax.all_to_all, axis_name="expert", split_axis=0, concat_axis=0, tiled=True
    )
    out_back = swap(out_rows.reshape(members, slot, width))
    d_hidden = spread_units(lambda: dot(weight_down, dy_rows, (((1,), (1,)), ((), ()))))
    d_gate_t = (d_hidden * up_t * sigma * (1.0 + gate_t * (1.0 - sigma))).astype(BF16)
    d_up_t = (d_hidden * active).astype(BF16)
    d_gate = lax.all_gather(d_gate_t, "tensor", axis=0, tiled=True)
    d_up = lax.all_gather(d_up_t, "tensor", axis=0, tiled=True)
    back_rows = (
        dot(d_gate, weight_gate, (((0,), (1,)), ((), ())))
        + dot(d_up, weight_up, (((0,), (1,)), ((), ())))
    ).astype(BF16)
    grad_w_gate = dot(x_rows, d_gate, (((0,), (1,)), ((), ()))).astype(BF16)[None]
    grad_w_up = dot(x_rows, d_up, (((0,), (1,)), ((), ()))).astype(BF16)[None]
    grad_w_down = dot(hidden, dy_rows, (((1,), (0,)), ((), ()))).astype(BF16)[None]
    grad_back = swap(back_rows.reshape(members, slot, width))
    mixed = dot(weighted, out_back.reshape(total, width), (((0,), (0,)), ((), ()))).astype(BF16)
    grad_tokens = dot(place, grad_back.reshape(total, width), (((0,), (0,)), ((), ()))).astype(BF16)
    return (mixed, grad_tokens, grad_w_gate, grad_w_up, grad_w_down)


NT = (((1,), (1,)), ((), ()))
TN = (((0,), (0,)), ((), ()))
NN = (((1,), (0,)), ((), ()))
VMEM = pl.BlockSpec(memory_space=pltpu.VMEM)
ANY = pl.BlockSpec(memory_space=pl.ANY)


def mm(a, b, dims=NN):
    return lax.dot_general(a, b, dims, preferred_element_type=F32)


def in_hbm(x):
    return pltpu.with_memory_space_constraint(x, pltpu.HBM)


def spec(shape, dtype=BF16):
    return jax.ShapeDtypeStruct(shape, dtype)


def call(kernel, outs, out_specs, ins, in_specs, scratch=(), after=(), flops=0, mib=16):
    late = len(after)

    def body(*refs):
        kernel(*refs[: len(ins)], *refs[len(ins) + late :])

    moved = sum(x.size * x.dtype.itemsize for x in (*ins, *outs))
    return pl.pallas_call(
        body,
        out_shape=list(outs),
        in_specs=list(in_specs) + [ANY] * late,
        out_specs=list(out_specs),
        scratch_shapes=list(scratch),
        compiler_params=pltpu.CompilerParams(vmem_limit_bytes=mib * 2**20),
        cost_estimate=pl.CostEstimate(flops=int(flops), bytes_accessed=int(moved), transcendentals=0),
    )(*ins, *after)


def placement(ids, members, slot, total):
    count = ids.shape[1]
    lanes = lax.broadcasted_iota(jnp.int32, (max(members, 8), count), 0)
    chosen = (lanes == ids).astype(F32)
    before = lax.broadcasted_iota(jnp.int32, (count, count), 0) < lax.broadcasted_iota(
        jnp.int32, (count, count), 1
    )
    ranks = mm(chosen.astype(BF16), before.astype(F32).astype(BF16))
    rank = jnp.sum(chosen * ranks, axis=0, keepdims=True).astype(jnp.int32)
    target = (ids ^ lax.axis_index("expert")) * slot + rank
    return lax.broadcasted_iota(jnp.int32, (total, count), 0) == target


def dispatch(ids, gates, tokens, cotangents, members, slot):
    (count, width), total = tokens.shape, members * slot
    ins = [ids, gates, tokens, cotangents]

    def kernel(*refs):
        sources, out_refs = refs[:4], refs[4 : 4 + 2 * members]
        held, sems = refs[4 + 2 * members : -1], refs[-1]
        copies = [
            pltpu.make_async_copy(s, h, sems.at[i]) for i, (s, h) in enumerate(zip(sources, held))
        ]
        for copy in copies:
            copy.start()
        copies[0].wait()
        copies[1].wait()
        mask = placement(held[0][...], members, slot, total)
        gate = held[1][...].astype(F32)
        for i, value in enumerate((1.0, gate)):
            pick = jnp.where(mask, value, 0.0).astype(BF16)
            copies[2 + i].wait()
            rows = mm(pick, held[2 + i][...]).astype(BF16)
            for m in range(members):
                out_refs[members * i + m][...] = rows[m * slot : (m + 1) * slot]

    out = call(
        kernel,
        [spec((slot, width))] * (2 * members),
        [VMEM] * (2 * members),
        [*map(in_hbm, ins)],
        [ANY] * 4,
        [pltpu.VMEM(x.shape, x.dtype) for x in ins] + [pltpu.SemaphoreType.DMA((4,))],
        (),
        4 * total * count * width,
    )
    return out[:members], out[members:]


def plan(ids, gates, members, slot, after=()):
    count, total = ids.shape[1], members * slot

    def kernel(ids_ref, gates_ref, plain, gated):
        mask = placement(ids_ref[...], members, slot, total)
        plain[...] = jnp.where(mask, 1.0, 0.0).T.astype(BF16)
        gated[...] = jnp.where(mask, gates_ref[...].astype(F32), 0.0).T.astype(BF16)

    return call(
        kernel, [spec((count, total))] * 2, [VMEM] * 2, [ids, gates], [VMEM, VMEM], (), after
    )


def collect(picks, rows):
    (count, total), (slot, width) = picks[0].shape, rows[0][0].shape
    n, members = len(picks), len(rows[0])

    def kernel(*refs):
        pick_refs, row_refs, out_refs = refs[:n], refs[n : n + n * members], refs[-n - 1 : -1]
        joined = refs[-1]
        for i in range(n):
            for m in range(members):
                joined[i, m * slot : (m + 1) * slot, :] = row_refs[i * members + m][...]
            out_refs[i][...] = mm(pick_refs[i][...], joined[i]).astype(BF16)

    return call(
        kernel,
        [spec((count, width))] * n,
        [VMEM] * n,
        [*picks, *(r for group in rows for r in group)],
        [VMEM] * (n + n * members),
        [pltpu.VMEM((n, total, width), BF16)],
        (),
        2 * n * count * total * width,
    )


def load(arrays, after=()):
    def kernel(*refs):
        n = len(arrays)
        copies = [
            pltpu.make_async_copy(refs[i], refs[n + i], refs[-1].at[i]) for i in range(n)
        ]
        for copy in copies:
            copy.start()
        for copy in copies:
            copy.wait()

    return call(
        kernel,
        [spec(x.shape, x.dtype) for x in arrays],
        [VMEM] * len(arrays),
        [in_hbm(x) for x in arrays],
        [ANY] * len(arrays),
        [pltpu.SemaphoreType.DMA((len(arrays),))],
        after,
    )


def block_of(ref, index, unit, axis):
    at = pl.ds(pl.multiple_of(index * unit, unit), unit)
    return ref[at, :] if axis == 0 else ref[:, at]


def away_terms(block, rows, weights, blocks, unit, down, after=()):
    members, (slot, width) = len(rows), rows[0].shape
    total, n = members * slot, len(weights)

    def kernel(*refs):
        row_refs, w_refs = refs[:members], refs[members : members + n]
        out_ref, joined = refs[-2:]
        for m, ref in enumerate(row_refs):
            joined[m * slot : (m + 1) * slot, :] = ref[...]
        x = joined[...]
        for j in range(blocks):
            for i, w_ref in enumerate(w_refs):
                w = block_of(w_ref, block(j), unit, 0 if down else 1)
                out_ref[j, i] = mm(x, w, NT if down else NN).astype(BF16)

    return call(
        kernel,
        [spec((blocks, n, total, unit)), spec((total, width))],
        [VMEM] * 2,
        [*rows, *weights],
        [VMEM] * (members + n),
        (),
        after,
        2 * n * blocks * total * width * unit,
    )


def kept_terms(block, joined, weights, arrived, unit, down, after=()):
    (total, width), n, blocks = joined.shape, len(weights), arrived.shape[0]
    first = blocks // 2

    def kernel(x_ref, *refs):
        w_refs, (got, send, keep) = refs[:n], refs[n:]
        x = x_ref[...]
        for j in (*range(first, blocks), *range(first)):
            for i, w_ref in enumerate(w_refs):
                w = block_of(w_ref, block(j), unit, 0 if down else 1)
                term = mm(x, w, NT if down else NN) + got[j, i].astype(F32)
                if j >= first:
                    send[j - first, i] = term.astype(BF16)
                else:
                    keep[j, i] = term

    return call(
        kernel,
        [spec((blocks - first, n, total, unit)), spec((first, n, total, unit), F32)],
        [VMEM] * 2,
        [joined, *weights, arrived],
        [VMEM] * (2 + n),
        (),
        after,
        2 * n * blocks * total * width * unit,
    )


def unit_rows(terms, unit, down, before=None, split=None, after=()):
    weights = [w for w, _ in terms]
    pieces = [(i, *piece) for i, (_, group) in enumerate(terms) for piece in group]
    units = [u for _, _, _, u in pieces]
    total = units[0].shape[2]
    width = weights[0].shape[1] if down else weights[0].shape[0]
    started = [] if before is None else [before]
    k, n = len(pieces), len(weights)

    def kernel(*refs):
        u_refs, w_refs, rest = refs[:k], refs[k : k + n], refs[k + n :]
        out_refs = rest[len(started) :]
        held, blocks = [], []
        for (i, block, first, _), u_ref in zip(pieces, u_refs):
            for j in range(u_ref.shape[0]):
                held.append(u_ref[j, 0])
                blocks.append(block_of(w_refs[i], block(first + j), unit, 0 if down else 1))
        acc = mm(
            jnp.concatenate(held, axis=1),
            jnp.concatenate(blocks, axis=0 if down else 1),
            NN if down else NT,
        )
        if started:
            acc = acc + rest[0][...]
        if split is None:
            out_refs[0][...] = acc
        else:
            for m, ref in enumerate(out_refs):
                ref[...] = acc[m * split : (m + 1) * split, :].astype(BF16)

    if split is None:
        outs = [spec((total, width), F32)]
    else:
        outs = [spec((split, width))] * (total // split)
    return call(
        kernel,
        outs,
        [VMEM] * len(outs),
        [*units, *weights, *started],
        [VMEM] * (k + n + len(started)),
        (),
        after,
        2 * sum(u.shape[0] for u in units) * total * width * unit,
    )


def weight_grads(groups, joined, unit, down, after=()):
    total, width = joined.shape
    pieces = [(i, *piece) for i, group in enumerate(groups) for piece in group]
    units = [u for _, _, _, u in pieces]
    k, n = len(pieces), len(groups)
    steps = sum(u.shape[0] for u in units)
    blocks = steps // n
    shape = (1, blocks * unit, width) if down else (1, width, blocks * unit)

    def kernel(*refs):
        u_refs, x_ref, out_refs = refs[:k], refs[k], refs[k + 1 :][:n]
        turned, held, sems = refs[-3:]
        if not down:
            turned[...] = x_ref[...].T
        waits = []
        for (i, block, first, _), u_ref in zip(pieces, u_refs):
            for j in range(u_ref.shape[0]):
                at = pl.ds(pl.multiple_of(block(first + j) * unit, unit), unit)
                slot = len(waits)
                if down:
                    held[slot] = mm(u_ref[j, 0], x_ref[...], TN).astype(BF16)
                    target = out_refs[i].at[0, at, :]
                else:
                    held[slot] = mm(turned[...], u_ref[j, 0]).astype(BF16)
                    target = out_refs[i].at[0, :, at]
                waits.append(pltpu.make_async_copy(held.at[slot], target, sems.at[slot]))
                waits[slot].start()
        for wait in waits:
            wait.wait()

    return call(
        kernel,
        [spec(shape)] * n,
        [ANY] * n,
        [*units, joined],
        [VMEM] * (k + 1),
        [
            pltpu.VMEM((8, 128) if down else (width, total), BF16),
            pltpu.VMEM((steps, unit, width) if down else (steps, width, unit), BF16),
            pltpu.SemaphoreType.DMA((steps,)),
        ],
        after,
        2 * steps * total * width * unit,
    )


def hop_orders(up, down):
    return (up, down), (up, down), (down, down), (down, down), (down, up)


def hypercube(tokens, gate_weights, expert_ids, w_gate, w_up, w_down, grad_out):
    members = lax.axis_size("expert")
    parts = lax.axis_size("tensor")
    bits = (parts // 2).bit_length() - 1
    count = tokens.shape[0]
    slot = 3 * count // (2 * members)
    unit = w_gate.shape[2] // parts
    half = parts // 2

    ids = expert_ids.reshape(1, count)
    gates = gate_weights.reshape(1, count)

    forward = tuple(range(bits))
    backward = forward[::-1]
    orders = dict(zip(("gu", "d", "h", "u", "g"), hop_orders(forward, backward)))

    def step_swap(x, step, name):
        pairs = [(d, d ^ (2 << orders[name][d % 2][step])) for d in range(parts)]
        return lax.ppermute(x, "tensor", pairs)

    def core_swap(x):
        return lax.ppermute(x, "tensor", [(d, d ^ 1) for d in range(parts)])

    def blocks_by(hops, other):
        def block(rel):
            t = lax.axis_index("tensor")
            core, chip = (t & 1) ^ other, t >> 1
            found = []
            for k in range(2):
                at = chip
                for step, bit in enumerate(hops[k]):
                    at = at ^ (((rel >> (bits - 1 - step)) & 1) << bit)
                index = jnp.int32(0)
                for bit in forward:
                    index = index * 2 + ((at >> bit) & 1)
                found.append(index)
            return half * core + jnp.where(core == 0, found[0], found[1])

        return block

    def halved(name):
        return blocks_by(orders[name], 0), blocks_by(orders[name], 1)

    def gathered(name):
        back = tuple(order[::-1] for order in orders[name])
        return blocks_by(back, 0), blocks_by(back, 1)

    def expert_swap(rows, skipped=0):
        out = []
        for m in range(1, members):
            pairs = [(d, d ^ m) for d in range(members)]
            out.append(lax.ppermute(rows[m - skipped], "expert", pairs))
        return out

    def halve(send, keep, name):
        size = send.shape[0]
        for step in range(bits):
            got = step_swap(send, step, name)
            total = keep + got.astype(F32)
            size //= 2
            if step < bits - 1:
                send, keep = total[size:].astype(BF16), total[:size]
        return total[0]

    def gather_units(x, name):
        for step in range(bits - 1):
            x = jnp.concatenate([x, step_swap(x, step, name)], axis=0)
        got = step_swap(x, bits - 1, name)
        mine, other = gathered(name)
        size = x.shape[0]
        early = ((mine, 0, x), (other, 0, core_swap(x)))
        late = ((mine, size, got), (other, size, core_swap(got)))
        return early, late

    x_slots, dy_slots = dispatch(ids, gates, tokens, grad_out, members, slot)
    x_rows = [x_slots[0]] + expert_swap(x_slots)
    weight_gate, weight_up, weight_down = load(
        (w_gate[0], w_up[0], w_down[0]), (x_slots[1],)
    )
    plain, gated = plan(ids, gates, members, slot, (weight_gate,))
    gate_up = (weight_gate, weight_up)
    dy_rows = [dy_slots[0]] + expert_swap(dy_slots)

    mine, other = halved("gu")
    away, x_all = away_terms(other, x_rows, gate_up, half, unit, False, (plain,))
    send, keep = kept_terms(mine, x_all, gate_up, core_swap(away), unit, False)
    mine, other = halved("d")
    away, dy_all = away_terms(other, dy_rows, (weight_down,), half, unit, True, (send,))
    gate, up = halve(send, keep, "gu")
    send, keep = kept_terms(mine, dy_all, (weight_down,), core_swap(away), unit, True)
    (d_hidden,) = halve(send, keep, "d")

    hidden = (gate * jax.nn.sigmoid(gate) * up).astype(BF16)
    hidden, gate, up = lax.optimization_barrier((hidden, gate, up))
    sigma = jax.nn.sigmoid(gate)
    active = gate * sigma
    d_gate = (d_hidden * up * sigma * (1.0 + gate * (1.0 - sigma))).astype(BF16)
    d_up = (d_hidden * active).astype(BF16)

    hidden_early, hidden_late = gather_units(hidden[None, None], "h")
    up_early, up_late = gather_units(d_up[None, None], "u")
    gate_early, gate_late = gather_units(d_gate[None, None], "g")
    hidden_all, up_all, gate_all = (
        hidden_early + hidden_late,
        up_early + up_late,
        gate_early + gate_late,
    )

    out = unit_rows(((weight_down, hidden_all),), unit, True, split=slot)
    out_back = expert_swap(out)
    (grad_w_down,) = weight_grads((hidden_all,), dy_all, unit, True, (out[0],))

    (part,) = unit_rows(((weight_up, up_all), (weight_gate, gate_early)), unit, False)
    back = unit_rows(((weight_gate, gate_late),), unit, False, part, slot)
    grad_back = expert_swap(back)
    grad_w_gate, grad_w_up = weight_grads((gate_all, up_all), x_all, unit, False, (back[0],))
    mixed, grad_tokens = collect(
        (gated, plain), ([out[0]] + out_back, [back[0]] + grad_back)
    )
    return (mixed, grad_tokens, grad_w_gate, grad_w_up, grad_w_down)


def power_of_two(n):
    return n & (n - 1) == 0


def solution(mesh):
    members, parts = mesh.shape["expert"], mesh.shape["tensor"]

    def local(*args):
        unit = args[3].shape[2] // parts
        slot = 3 * args[0].shape[0] // (2 * members)
        fits = power_of_two(members) and power_of_two(parts) and parts >= 4
        fits = fits and unit % 128 == 0 and slot % 16 == 0 and args[0].shape[1] % 128 == 0
        fits = fits and args[2].shape[1] == 1
        return (hypercube if fits else general)(*args)

    in_specs = (
        P("expert", "tensor"),
        P("expert", None),
        P("expert", None),
        P("expert", "tensor", None),
        P("expert", "tensor", None),
        P("expert", None, "tensor"),
        P("expert", "tensor"),
    )
    out_specs = (
        P("expert", "tensor"),
        P("expert", "tensor"),
        P("expert", "tensor", None),
        P("expert", "tensor", None),
        P("expert", None, "tensor"),
    )
    return jax.shard_map(local, mesh=mesh, in_specs=in_specs, out_specs=out_specs, check_vma=False)
```

```python
import functools

import jax
import jax.numpy as jnp
from jax import lax
from jax.experimental import pallas as pl
from jax.experimental.pallas import tpu as pltpu
from jax.sharding import PartitionSpec as P


F32 = jnp.float32
BF16 = jnp.bfloat16


def spread_units(function):
    return lax.psum_scatter(function(), "tensor", scatter_dimension=0, tiled=True)


def general(tokens, gate_weights, expert_ids, w_gate, w_up, w_down, grad_out):
    members = lax.axis_size("expert")
    tok_rows = tokens.shape[0]
    routes = expert_ids.shape[1]
    width = tokens.shape[1]
    slot = 3 * routes * tok_rows // (2 * members)
    total = members * slot
    flat_ids = expert_ids.reshape(-1)
    counted = (flat_ids[:, None] == jnp.arange(members, dtype=jnp.int32)[None, :]).astype(jnp.int32)
    ranks = jnp.cumsum(counted, axis=0) - 1
    position = jnp.sum(counted * ranks, axis=1)
    target = (flat_ids * slot + position).reshape(tok_rows, routes)
    matched = target[None, :, :] == jnp.arange(total, dtype=jnp.int32)[:, None, None]
    place = jnp.sum(matched.astype(F32), axis=2).astype(BF16)
    weighted = jnp.sum(jnp.where(matched, gate_weights.astype(F32)[None], 0.0), axis=2).astype(BF16)
    x_slots = jnp.dot(place, tokens, preferred_element_type=F32).astype(BF16)
    dy_slots = jnp.dot(weighted, grad_out, preferred_element_type=F32).astype(BF16)
    outgoing = jnp.stack(
        [x_slots.reshape(members, slot, width), dy_slots.reshape(members, slot, width)], axis=1
    )
    arrived = lax.all_to_all(outgoing, "expert", split_axis=0, concat_axis=0, tiled=True)
    x_rows = arrived[:, 0].reshape(total, width)
    dy_rows = arrived[:, 1].reshape(total, width)
    weight_gate, weight_up, weight_down = w_gate[0], w_up[0], w_down[0]
    dot = functools.partial(lax.dot_general, preferred_element_type=F32)

    def gate_terms():
        return jnp.concatenate(
            [dot(w, x_rows, (((0,), (1,)), ((), ()))) for w in (weight_gate, weight_up)], axis=1
        )

    summed = spread_units(gate_terms)
    gate_t, up_t = summed[:, :total], summed[:, total:]
    sigma = jax.nn.sigmoid(gate_t)
    active = gate_t * sigma
    hidden_t = (active * up_t).astype(BF16)
    hidden = lax.all_gather(hidden_t, "tensor", axis=0, tiled=True)
    out_rows = dot(hidden, weight_down, (((0,), (0,)), ((), ()))).astype(BF16)
    swap = functools.partial(
        lax.all_to_all, axis_name="expert", split_axis=0, concat_axis=0, tiled=True
    )
    out_back = swap(out_rows.reshape(members, slot, width))
    d_hidden = spread_units(lambda: dot(weight_down, dy_rows, (((1,), (1,)), ((), ()))))
    d_gate_t = (d_hidden * up_t * sigma * (1.0 + gate_t * (1.0 - sigma))).astype(BF16)
    d_up_t = (d_hidden * active).astype(BF16)
    d_gate = lax.all_gather(d_gate_t, "tensor", axis=0, tiled=True)
    d_up = lax.all_gather(d_up_t, "tensor", axis=0, tiled=True)
    back_rows = (
        dot(d_gate, weight_gate, (((0,), (1,)), ((), ())))
        + dot(d_up, weight_up, (((0,), (1,)), ((), ())))
    ).astype(BF16)
    grad_w_gate = dot(x_rows, d_gate, (((0,), (1,)), ((), ()))).astype(BF16)[None]
    grad_w_up = dot(x_rows, d_up, (((0,), (1,)), ((), ()))).astype(BF16)[None]
    grad_w_down = dot(hidden, dy_rows, (((1,), (0,)), ((), ()))).astype(BF16)[None]
    grad_back = swap(back_rows.reshape(members, slot, width))
    mixed = dot(weighted, out_back.reshape(total, width), (((0,), (0,)), ((), ()))).astype(BF16)
    grad_tokens = dot(place, grad_back.reshape(total, width), (((0,), (0,)), ((), ()))).astype(BF16)
    return (mixed, grad_tokens, grad_w_gate, grad_w_up, grad_w_down)


NT = (((1,), (1,)), ((), ()))
TN = (((0,), (0,)), ((), ()))
NN = (((1,), (0,)), ((), ()))
VMEM = pl.BlockSpec(memory_space=pltpu.VMEM)
ANY = pl.BlockSpec(memory_space=pl.ANY)


def mm(a, b, dims=NN):
    return lax.dot_general(a, b, dims, preferred_element_type=F32)


def in_hbm(x):
    return pltpu.with_memory_space_constraint(x, pltpu.HBM)


def spec(shape, dtype=BF16):
    return jax.ShapeDtypeStruct(shape, dtype)


def call(
    kernel, outs, out_specs, ins, in_specs, scratch=(), after=(), flops=0, aliases=None, mib=16
):
    late = len(after)

    def body(*refs):
        kernel(*refs[: len(ins)], *refs[len(ins) + late :])

    moved = sum(x.size * x.dtype.itemsize for x in (*ins, *outs))
    return pl.pallas_call(
        body,
        out_shape=list(outs),
        in_specs=list(in_specs) + [ANY] * late,
        out_specs=list(out_specs),
        scratch_shapes=list(scratch),
        input_output_aliases=aliases or {},
        compiler_params=pltpu.CompilerParams(vmem_limit_bytes=mib * 2**20),
        cost_estimate=pl.CostEstimate(flops=int(flops), bytes_accessed=int(moved), transcendentals=0),
    )(*ins, *after)


def placement(ids, members, slot, total):
    count = ids.shape[1]
    lanes = lax.broadcasted_iota(jnp.int32, (max(members, 8), count), 0)
    chosen = (lanes == ids).astype(F32)
    before = lax.broadcasted_iota(jnp.int32, (count, count), 0) < lax.broadcasted_iota(
        jnp.int32, (count, count), 1
    )
    ranks = mm(chosen.astype(BF16), before.astype(F32).astype(BF16))
    rank = jnp.sum(chosen * ranks, axis=0, keepdims=True).astype(jnp.int32)
    target = (ids ^ lax.axis_index("expert")) * slot + rank
    return lax.broadcasted_iota(jnp.int32, (total, count), 0) == target


def dispatch(ids, gates, tokens, cotangents, members, slot):
    (count, width), total = tokens.shape, members * slot
    ins = [ids, gates, tokens, cotangents]

    def kernel(*refs):
        sources, out_refs = refs[:4], refs[4 : 4 + 2 * members]
        held, sems = refs[4 + 2 * members : -1], refs[-1]
        copies = [
            pltpu.make_async_copy(s, h, sems.at[i]) for i, (s, h) in enumerate(zip(sources, held))
        ]
        for copy in copies:
            copy.start()
        copies[0].wait()
        copies[1].wait()
        mask = placement(held[0][...], members, slot, total)
        gate = held[1][...].astype(F32)
        for i, value in enumerate((1.0, gate)):
            pick = jnp.where(mask, value, 0.0).astype(BF16)
            copies[2 + i].wait()
            rows = mm(pick, held[2 + i][...]).astype(BF16)
            for m in range(members):
                out_refs[members * i + m][...] = rows[m * slot : (m + 1) * slot]

    out = call(
        kernel,
        [spec((slot, width))] * (2 * members),
        [VMEM] * (2 * members),
        [*map(in_hbm, ins)],
        [ANY] * 4,
        [pltpu.VMEM(x.shape, x.dtype) for x in ins] + [pltpu.SemaphoreType.DMA((4,))],
        (),
        4 * total * count * width,
    )
    return out[:members], out[members:]


def plan(ids, gates, members, slot, after=()):
    count, total = ids.shape[1], members * slot

    def kernel(ids_ref, gates_ref, plain, gated):
        mask = placement(ids_ref[...], members, slot, total)
        plain[...] = jnp.where(mask, 1.0, 0.0).T.astype(BF16)
        gated[...] = jnp.where(mask, gates_ref[...].astype(F32), 0.0).T.astype(BF16)

    return call(
        kernel, [spec((count, total))] * 2, [VMEM] * 2, [ids, gates], [VMEM, VMEM], (), after
    )


def collect(picks, rows):
    (count, total), (slot, width) = picks[0].shape, rows[0][0].shape
    n, members = len(picks), len(rows[0])

    def kernel(*refs):
        pick_refs, row_refs, out_refs = refs[:n], refs[n : n + n * members], refs[-n - 1 : -1]
        joined = refs[-1]
        for i in range(n):
            for m in range(members):
                joined[i, m * slot : (m + 1) * slot, :] = row_refs[i * members + m][...]
            out_refs[i][...] = mm(pick_refs[i][...], joined[i]).astype(BF16)

    return call(
        kernel,
        [spec((count, width))] * n,
        [VMEM] * n,
        [*picks, *(r for group in rows for r in group)],
        [VMEM] * (n + n * members),
        [pltpu.VMEM((n, total, width), BF16)],
        (),
        2 * n * count * total * width,
    )


def load(arrays, after=()):
    def kernel(*refs):
        n = len(arrays)
        copies = [
            pltpu.make_async_copy(refs[i], refs[n + i], refs[-1].at[i]) for i in range(n)
        ]
        for copy in copies:
            copy.start()
        for copy in copies:
            copy.wait()

    return call(
        kernel,
        [spec(x.shape, x.dtype) for x in arrays],
        [VMEM] * len(arrays),
        [in_hbm(x) for x in arrays],
        [ANY] * len(arrays),
        [pltpu.SemaphoreType.DMA((len(arrays),))],
        after,
    )


def block_of(ref, index, unit, axis):
    at = pl.ds(pl.multiple_of(index * unit, unit), unit)
    return ref[at, :] if axis == 0 else ref[:, at]


def away_terms(block, rows, weights, blocks, unit, down, after=()):
    members, (slot, width) = len(rows), rows[0].shape
    total, n = members * slot, len(weights)

    def kernel(*refs):
        row_refs, w_refs = refs[:members], refs[members : members + n]
        out_ref, joined = refs[-2:]
        for m, ref in enumerate(row_refs):
            joined[m * slot : (m + 1) * slot, :] = ref[...]
        x = joined[...]
        for j in range(blocks):
            for i, w_ref in enumerate(w_refs):
                w = block_of(w_ref, block(j), unit, 0 if down else 1)
                out_ref[j, i] = mm(x, w, NT if down else NN).astype(BF16)

    return call(
        kernel,
        [spec((blocks, n, total, unit)), spec((total, width))],
        [VMEM] * 2,
        [*rows, *weights],
        [VMEM] * (members + n),
        (),
        after,
        2 * n * blocks * total * width * unit,
    )


def kept_terms(block, joined, weights, arrived, unit, down, after=()):
    (total, width), n, blocks = joined.shape, len(weights), arrived.shape[0]
    first = blocks // 2

    def kernel(x_ref, *refs):
        w_refs, (got, send, keep) = refs[:n], refs[n:]
        x = x_ref[...]
        for j in (*range(first, blocks), *range(first)):
            for i, w_ref in enumerate(w_refs):
                w = block_of(w_ref, block(j), unit, 0 if down else 1)
                term = mm(x, w, NT if down else NN) + got[j, i].astype(F32)
                if j >= first:
                    send[j - first, i] = term.astype(BF16)
                else:
                    keep[j, i] = term

    return call(
        kernel,
        [spec((blocks - first, n, total, unit)), spec((first, n, total, unit), F32)],
        [VMEM] * 2,
        [joined, *weights, arrived],
        [VMEM] * (2 + n),
        (),
        after,
        2 * n * blocks * total * width * unit,
    )


def unit_rows(terms, unit, down, before=None, split=None, after=()):
    weights = [w for w, _ in terms]
    pieces = [(i, *piece) for i, (_, group) in enumerate(terms) for piece in group]
    units = [u for _, _, _, u in pieces]
    total = units[0].shape[2]
    width = weights[0].shape[1] if down else weights[0].shape[0]
    started = [] if before is None else [before]
    k, n = len(pieces), len(weights)

    def kernel(*refs):
        u_refs, w_refs, rest = refs[:k], refs[k : k + n], refs[k + n :]
        out_refs = rest[len(started) :]
        held, blocks = [], []
        for (i, block, first, _), u_ref in zip(pieces, u_refs):
            for j in range(u_ref.shape[0]):
                held.append(u_ref[j, 0])
                blocks.append(block_of(w_refs[i], block(first + j), unit, 0 if down else 1))
        acc = mm(
            jnp.concatenate(held, axis=1),
            jnp.concatenate(blocks, axis=0 if down else 1),
            NN if down else NT,
        )
        if started:
            acc = acc + rest[0][...]
        if split is None:
            out_refs[0][...] = acc
        else:
            for m, ref in enumerate(out_refs):
                ref[...] = acc[m * split : (m + 1) * split, :].astype(BF16)

    if split is None:
        outs = [spec((total, width), F32)]
    else:
        outs = [spec((split, width))] * (total // split)
    return call(
        kernel,
        outs,
        [VMEM] * len(outs),
        [*units, *weights, *started],
        [VMEM] * (k + n + len(started)),
        (),
        after,
        2 * sum(u.shape[0] for u in units) * total * width * unit,
    )


def weight_grads(groups, joined, unit, count, down, onto=(), after=()):
    total, width = joined.shape
    pieces = [(i, *piece) for i, group in enumerate(groups) for piece in group]
    units = [u for _, _, _, u in pieces]
    k, n = len(pieces), len(groups)
    steps = sum(u.shape[0] for u in units)
    shape = (1, count * unit, width) if down else (1, width, count * unit)

    def kernel(*refs):
        u_refs, x_ref = refs[:k], refs[k]
        out_refs = refs[k + 1 + len(onto) :][:n]
        turned, held, sems = refs[-3:]
        if not down:
            turned[...] = x_ref[...].T
        waits = []
        for (i, block, first, _), u_ref in zip(pieces, u_refs):
            for j in range(u_ref.shape[0]):
                at = pl.ds(pl.multiple_of(block(first + j) * unit, unit), unit)
                slot = len(waits)
                if down:
                    held[slot] = mm(u_ref[j, 0], x_ref[...], TN).astype(BF16)
                    target = out_refs[i].at[0, at, :]
                else:
                    held[slot] = mm(turned[...], u_ref[j, 0]).astype(BF16)
                    target = out_refs[i].at[0, :, at]
                waits.append(pltpu.make_async_copy(held.at[slot], target, sems.at[slot]))
                waits[slot].start()
        for wait in waits:
            wait.wait()

    return call(
        kernel,
        [spec(shape)] * n,
        [ANY] * n,
        [*units, joined, *onto],
        [VMEM] * (k + 1) + [ANY] * len(onto),
        [
            pltpu.VMEM((8, 128) if down else (width, total), BF16),
            pltpu.VMEM((steps, unit, width) if down else (steps, width, unit), BF16),
            pltpu.SemaphoreType.DMA((steps,)),
        ],
        after,
        2 * steps * total * width * unit,
        {k + 1 + i: n - len(onto) + i for i in range(len(onto))},
    )


def hop_orders(up, down):
    return (up, down), (up, down), (down, down), (down, up), (down, down)


def hypercube(tokens, gate_weights, expert_ids, w_gate, w_up, w_down, grad_out):
    members = lax.axis_size("expert")
    parts = lax.axis_size("tensor")
    bits = (parts // 2).bit_length() - 1
    count = tokens.shape[0]
    slot = 3 * count // (2 * members)
    unit = w_gate.shape[2] // parts
    half = parts // 2

    ids = expert_ids.reshape(1, count)
    gates = gate_weights.reshape(1, count)

    forward = tuple(range(bits))
    backward = forward[::-1]
    orders = dict(zip(("gu", "d", "h", "u", "g"), hop_orders(forward, backward)))

    def step_swap(x, step, name):
        pairs = [(d, d ^ (2 << orders[name][d % 2][step])) for d in range(parts)]
        return lax.ppermute(x, "tensor", pairs)

    def core_swap(x):
        return lax.ppermute(x, "tensor", [(d, d ^ 1) for d in range(parts)])

    def blocks_by(hops, other):
        def block(rel):
            t = lax.axis_index("tensor")
            core, chip = (t & 1) ^ other, t >> 1
            found = []
            for k in range(2):
                at = chip
                for step, bit in enumerate(hops[k]):
                    at = at ^ (((rel >> (bits - 1 - step)) & 1) << bit)
                index = jnp.int32(0)
                for bit in forward:
                    index = index * 2 + ((at >> bit) & 1)
                found.append(index)
            return half * core + jnp.where(core == 0, found[0], found[1])

        return block

    def halved(name):
        return blocks_by(orders[name], 0), blocks_by(orders[name], 1)

    def gathered(name):
        back = tuple(order[::-1] for order in orders[name])
        return blocks_by(back, 0), blocks_by(back, 1)

    def expert_swap(rows, skipped=0):
        out = []
        for m in range(1, members):
            pairs = [(d, d ^ m) for d in range(members)]
            out.append(lax.ppermute(rows[m - skipped], "expert", pairs))
        return out

    def halve(send, keep, name):
        size = send.shape[0]
        for step in range(bits):
            got = step_swap(send, step, name)
            total = keep + got.astype(F32)
            size //= 2
            if step < bits - 1:
                send, keep = total[size:].astype(BF16), total[:size]
        return total[0]

    def gather_units(x, name):
        for step in range(bits - 1):
            x = jnp.concatenate([x, step_swap(x, step, name)], axis=0)
        got = step_swap(x, bits - 1, name)
        mine, other = gathered(name)
        size = x.shape[0]
        early = ((mine, 0, x), (other, 0, core_swap(x)))
        late = ((mine, size, got), (other, size, core_swap(got)))
        return early, late

    x_slots, dy_slots = dispatch(ids, gates, tokens, grad_out, members, slot)
    x_rows = [x_slots[0]] + expert_swap(x_slots)
    weight_gate, weight_up, weight_down = load(
        (w_gate[0], w_up[0], w_down[0]), (x_slots[1],)
    )
    plain, gated = plan(ids, gates, members, slot, (weight_gate,))
    gate_up = (weight_gate, weight_up)
    dy_rows = [dy_slots[0]] + expert_swap(dy_slots)

    mine, other = halved("gu")
    away, x_all = away_terms(other, x_rows, gate_up, half, unit, False)
    send, keep = kept_terms(mine, x_all, gate_up, core_swap(away), unit, False)
    mine, other = halved("d")
    away, dy_all = away_terms(other, dy_rows, (weight_down,), half, unit, True, (send,))
    gate, up = halve(send, keep, "gu")
    send, keep = kept_terms(mine, dy_all, (weight_down,), core_swap(away), unit, True)
    (d_hidden,) = halve(send, keep, "d")

    hidden = (gate * jax.nn.sigmoid(gate) * up).astype(BF16)
    hidden, gate, up = lax.optimization_barrier((hidden, gate, up))
    sigma = jax.nn.sigmoid(gate)
    active = gate * sigma
    d_gate = (d_hidden * up * sigma * (1.0 + gate * (1.0 - sigma))).astype(BF16)
    d_up = (d_hidden * active).astype(BF16)

    hidden_early, hidden_late = gather_units(hidden[None, None], "h")
    up_early, up_late = gather_units(d_up[None, None], "u")
    gate_early, gate_late = gather_units(d_gate[None, None], "g")
    gate_all = gate_early + gate_late

    (part,) = unit_rows(((weight_down, hidden_early),), unit, True)
    out = unit_rows(((weight_down, hidden_late),), unit, True, part, slot)
    out_back = expert_swap(out)
    grad_w_down = weight_grads((hidden_early,), dy_all, unit, parts, True)
    (grad_w_down,) = weight_grads((hidden_late,), dy_all, unit, parts, True, grad_w_down)

    (part,) = unit_rows(((weight_up, up_early),), unit, False)
    (part,) = unit_rows(((weight_up, up_late), (weight_gate, gate_early)), unit, False, part)
    back = unit_rows(((weight_gate, gate_late),), unit, False, part, slot)
    grad_back = expert_swap(back)
    grad_w_up = weight_grads((up_early,), x_all, unit, parts, False)
    grad_w_gate, grad_w_up = weight_grads((gate_all, up_late), x_all, unit, parts, False, grad_w_up)
    mixed, grad_tokens = collect(
        (gated, plain), ([out[0]] + out_back, [back[0]] + grad_back)
    )
    return (mixed, grad_tokens, grad_w_gate, grad_w_up, grad_w_down)


def power_of_two(n):
    return n & (n - 1) == 0


def solution(mesh):
    members, parts = mesh.shape["expert"], mesh.shape["tensor"]

    def local(*args):
        unit = args[3].shape[2] // parts
        slot = 3 * args[0].shape[0] // (2 * members)
        fits = power_of_two(members) and power_of_two(parts) and parts >= 4
        fits = fits and unit % 128 == 0 and slot % 16 == 0 and args[0].shape[1] % 128 == 0
        fits = fits and args[2].shape[1] == 1
        return (hypercube if fits else general)(*args)

    in_specs = (
        P("expert", "tensor"),
        P("expert", None),
        P("expert", None),
        P("expert", "tensor", None),
        P("expert", "tensor", None),
        P("expert", None, "tensor"),
        P("expert", "tensor"),
    )
    out_specs = (
        P("expert", "tensor"),
        P("expert", "tensor"),
        P("expert", "tensor", None),
        P("expert", "tensor", None),
        P("expert", None, "tensor"),
    )
    return jax.shard_map(local, mesh=mesh, in_specs=in_specs, out_specs=out_specs, check_vma=False)
```

```python
import functools

import jax
import jax.numpy as jnp
from jax import lax
from jax.experimental import pallas as pl
from jax.experimental.pallas import tpu as pltpu
from jax.sharding import PartitionSpec as P


F32 = jnp.float32
BF16 = jnp.bfloat16


def spread_units(function):
    return lax.psum_scatter(function(), "tensor", scatter_dimension=0, tiled=True)


def general(tokens, gate_weights, expert_ids, w_gate, w_up, w_down, grad_out):
    members = lax.axis_size("expert")
    tok_rows = tokens.shape[0]
    routes = expert_ids.shape[1]
    width = tokens.shape[1]
    slot = 3 * routes * tok_rows // (2 * members)
    total = members * slot
    flat_ids = expert_ids.reshape(-1)
    counted = (flat_ids[:, None] == jnp.arange(members, dtype=jnp.int32)[None, :]).astype(jnp.int32)
    ranks = jnp.cumsum(counted, axis=0) - 1
    position = jnp.sum(counted * ranks, axis=1)
    target = (flat_ids * slot + position).reshape(tok_rows, routes)
    matched = target[None, :, :] == jnp.arange(total, dtype=jnp.int32)[:, None, None]
    place = jnp.sum(matched.astype(F32), axis=2).astype(BF16)
    weighted = jnp.sum(jnp.where(matched, gate_weights.astype(F32)[None], 0.0), axis=2).astype(BF16)
    x_slots = jnp.dot(place, tokens, preferred_element_type=F32).astype(BF16)
    dy_slots = jnp.dot(weighted, grad_out, preferred_element_type=F32).astype(BF16)
    outgoing = jnp.stack(
        [x_slots.reshape(members, slot, width), dy_slots.reshape(members, slot, width)], axis=1
    )
    arrived = lax.all_to_all(outgoing, "expert", split_axis=0, concat_axis=0, tiled=True)
    x_rows = arrived[:, 0].reshape(total, width)
    dy_rows = arrived[:, 1].reshape(total, width)
    weight_gate, weight_up, weight_down = w_gate[0], w_up[0], w_down[0]
    dot = functools.partial(lax.dot_general, preferred_element_type=F32)

    def gate_terms():
        return jnp.concatenate(
            [dot(w, x_rows, (((0,), (1,)), ((), ()))) for w in (weight_gate, weight_up)], axis=1
        )

    summed = spread_units(gate_terms)
    gate_t, up_t = summed[:, :total], summed[:, total:]
    sigma = jax.nn.sigmoid(gate_t)
    active = gate_t * sigma
    hidden_t = (active * up_t).astype(BF16)
    hidden = lax.all_gather(hidden_t, "tensor", axis=0, tiled=True)
    out_rows = dot(hidden, weight_down, (((0,), (0,)), ((), ()))).astype(BF16)
    swap = functools.partial(
        lax.all_to_all, axis_name="expert", split_axis=0, concat_axis=0, tiled=True
    )
    out_back = swap(out_rows.reshape(members, slot, width))
    d_hidden = spread_units(lambda: dot(weight_down, dy_rows, (((1,), (1,)), ((), ()))))
    d_gate_t = (d_hidden * up_t * sigma * (1.0 + gate_t * (1.0 - sigma))).astype(BF16)
    d_up_t = (d_hidden * active).astype(BF16)
    d_gate = lax.all_gather(d_gate_t, "tensor", axis=0, tiled=True)
    d_up = lax.all_gather(d_up_t, "tensor", axis=0, tiled=True)
    back_rows = (
        dot(d_gate, weight_gate, (((0,), (1,)), ((), ())))
        + dot(d_up, weight_up, (((0,), (1,)), ((), ())))
    ).astype(BF16)
    grad_w_gate = dot(x_rows, d_gate, (((0,), (1,)), ((), ()))).astype(BF16)[None]
    grad_w_up = dot(x_rows, d_up, (((0,), (1,)), ((), ()))).astype(BF16)[None]
    grad_w_down = dot(hidden, dy_rows, (((1,), (0,)), ((), ()))).astype(BF16)[None]
    grad_back = swap(back_rows.reshape(members, slot, width))
    mixed = dot(weighted, out_back.reshape(total, width), (((0,), (0,)), ((), ()))).astype(BF16)
    grad_tokens = dot(place, grad_back.reshape(total, width), (((0,), (0,)), ((), ()))).astype(BF16)
    return (mixed, grad_tokens, grad_w_gate, grad_w_up, grad_w_down)


NT = (((1,), (1,)), ((), ()))
TN = (((0,), (0,)), ((), ()))
NN = (((1,), (0,)), ((), ()))
VMEM = pl.BlockSpec(memory_space=pltpu.VMEM)
ANY = pl.BlockSpec(memory_space=pl.ANY)


def mm(a, b, dims=NN):
    return lax.dot_general(a, b, dims, preferred_element_type=F32)


def in_hbm(x):
    return pltpu.with_memory_space_constraint(x, pltpu.HBM)


def spec(shape, dtype=BF16):
    return jax.ShapeDtypeStruct(shape, dtype)


def call(
    kernel, outs, out_specs, ins, in_specs, scratch=(), after=(), flops=0, aliases=None, mib=16
):
    late = len(after)

    def body(*refs):
        kernel(*refs[: len(ins)], *refs[len(ins) + late :])

    moved = sum(x.size * x.dtype.itemsize for x in (*ins, *outs))
    return pl.pallas_call(
        body,
        out_shape=list(outs),
        in_specs=list(in_specs) + [ANY] * late,
        out_specs=list(out_specs),
        scratch_shapes=list(scratch),
        input_output_aliases=aliases or {},
        compiler_params=pltpu.CompilerParams(vmem_limit_bytes=mib * 2**20),
        cost_estimate=pl.CostEstimate(flops=int(flops), bytes_accessed=int(moved), transcendentals=0),
    )(*ins, *after)


def placement(ids, members, slot, total):
    count = ids.shape[1]
    lanes = lax.broadcasted_iota(jnp.int32, (max(members, 8), count), 0)
    chosen = (lanes == ids).astype(F32)
    before = lax.broadcasted_iota(jnp.int32, (count, count), 0) < lax.broadcasted_iota(
        jnp.int32, (count, count), 1
    )
    ranks = mm(chosen.astype(BF16), before.astype(F32).astype(BF16))
    rank = jnp.sum(chosen * ranks, axis=0, keepdims=True).astype(jnp.int32)
    target = (ids ^ lax.axis_index("expert")) * slot + rank
    return lax.broadcasted_iota(jnp.int32, (total, count), 0) == target


def dispatch(ids, gates, tokens, cotangents, members, slot):
    (count, width), total = tokens.shape, members * slot
    ins = [ids, gates, tokens, cotangents]

    def kernel(*refs):
        sources, out_refs = refs[:4], refs[4 : 4 + 2 * members]
        held, sems = refs[4 + 2 * members : -1], refs[-1]
        copies = [
            pltpu.make_async_copy(s, h, sems.at[i]) for i, (s, h) in enumerate(zip(sources, held))
        ]
        for copy in copies:
            copy.start()
        copies[0].wait()
        copies[1].wait()
        mask = placement(held[0][...], members, slot, total)
        gate = held[1][...].astype(F32)
        for i, value in enumerate((1.0, gate)):
            pick = jnp.where(mask, value, 0.0).astype(BF16)
            copies[2 + i].wait()
            rows = mm(pick, held[2 + i][...]).astype(BF16)
            for m in range(members):
                out_refs[members * i + m][...] = rows[m * slot : (m + 1) * slot]

    out = call(
        kernel,
        [spec((slot, width))] * (2 * members),
        [VMEM] * (2 * members),
        [*map(in_hbm, ins)],
        [ANY] * 4,
        [pltpu.VMEM(x.shape, x.dtype) for x in ins] + [pltpu.SemaphoreType.DMA((4,))],
        (),
        4 * total * count * width,
    )
    return out[:members], out[members:]


def plan(ids, gates, members, slot, after=()):
    count, total = ids.shape[1], members * slot

    def kernel(ids_ref, gates_ref, plain, gated):
        mask = placement(ids_ref[...], members, slot, total)
        plain[...] = jnp.where(mask, 1.0, 0.0).T.astype(BF16)
        gated[...] = jnp.where(mask, gates_ref[...].astype(F32), 0.0).T.astype(BF16)

    return call(
        kernel, [spec((count, total))] * 2, [VMEM] * 2, [ids, gates], [VMEM, VMEM], (), after
    )


def collect(picks, rows):
    (count, total), (slot, width) = picks[0].shape, rows[0][0].shape
    n, members = len(picks), len(rows[0])

    def kernel(*refs):
        pick_refs, row_refs, out_refs = refs[:n], refs[n : n + n * members], refs[-n - 1 : -1]
        joined = refs[-1]
        for i in range(n):
            for m in range(members):
                joined[i, m * slot : (m + 1) * slot, :] = row_refs[i * members + m][...]
            out_refs[i][...] = mm(pick_refs[i][...], joined[i]).astype(BF16)

    return call(
        kernel,
        [spec((count, width))] * n,
        [VMEM] * n,
        [*picks, *(r for group in rows for r in group)],
        [VMEM] * (n + n * members),
        [pltpu.VMEM((n, total, width), BF16)],
        (),
        2 * n * count * total * width,
    )


def load(arrays, after=()):
    def kernel(*refs):
        n = len(arrays)
        copies = [
            pltpu.make_async_copy(refs[i], refs[n + i], refs[-1].at[i]) for i in range(n)
        ]
        for copy in copies:
            copy.start()
        for copy in copies:
            copy.wait()

    return call(
        kernel,
        [spec(x.shape, x.dtype) for x in arrays],
        [VMEM] * len(arrays),
        [in_hbm(x) for x in arrays],
        [ANY] * len(arrays),
        [pltpu.SemaphoreType.DMA((len(arrays),))],
        after,
    )


def block_of(ref, index, unit, axis):
    at = pl.ds(pl.multiple_of(index * unit, unit), unit)
    return ref[at, :] if axis == 0 else ref[:, at]


def away_terms(block, rows, weights, blocks, unit, down, after=()):
    members, (slot, width) = len(rows), rows[0].shape
    total, n = members * slot, len(weights)

    def kernel(*refs):
        row_refs, w_refs = refs[:members], refs[members : members + n]
        out_ref, joined = refs[-2:]
        for m, ref in enumerate(row_refs):
            joined[m * slot : (m + 1) * slot, :] = ref[...]
        x = joined[...]
        for j in range(blocks):
            for i, w_ref in enumerate(w_refs):
                w = block_of(w_ref, block(j), unit, 0 if down else 1)
                out_ref[j, i] = mm(x, w, NT if down else NN).astype(BF16)

    return call(
        kernel,
        [spec((blocks, n, total, unit)), spec((total, width))],
        [VMEM] * 2,
        [*rows, *weights],
        [VMEM] * (members + n),
        (),
        after,
        2 * n * blocks * total * width * unit,
    )


def kept_terms(block, joined, weights, arrived, unit, down, after=()):
    (total, width), n, blocks = joined.shape, len(weights), arrived.shape[0]
    first = blocks // 2

    def kernel(x_ref, *refs):
        w_refs, (got, send, keep) = refs[:n], refs[n:]
        x = x_ref[...]
        for j in (*range(first, blocks), *range(first)):
            for i, w_ref in enumerate(w_refs):
                w = block_of(w_ref, block(j), unit, 0 if down else 1)
                term = mm(x, w, NT if down else NN) + got[j, i].astype(F32)
                if j >= first:
                    send[j - first, i] = term.astype(BF16)
                else:
                    keep[j, i] = term

    return call(
        kernel,
        [spec((blocks - first, n, total, unit)), spec((first, n, total, unit), F32)],
        [VMEM] * 2,
        [joined, *weights, arrived],
        [VMEM] * (2 + n),
        (),
        after,
        2 * n * blocks * total * width * unit,
    )


def unit_rows(terms, unit, down, before=None, split=None, after=()):
    weights = [w for w, _ in terms]
    pieces = [(i, *piece) for i, (_, group) in enumerate(terms) for piece in group]
    units = [u for _, _, _, u in pieces]
    total = units[0].shape[2]
    width = weights[0].shape[1] if down else weights[0].shape[0]
    started = [] if before is None else [before]
    k, n = len(pieces), len(weights)

    def kernel(*refs):
        u_refs, w_refs, rest = refs[:k], refs[k : k + n], refs[k + n :]
        out_refs = rest[len(started) :]
        held, blocks = [], []
        for (i, block, first, _), u_ref in zip(pieces, u_refs):
            for j in range(u_ref.shape[0]):
                held.append(u_ref[j, 0])
                blocks.append(block_of(w_refs[i], block(first + j), unit, 0 if down else 1))
        acc = mm(
            jnp.concatenate(held, axis=1),
            jnp.concatenate(blocks, axis=0 if down else 1),
            NN if down else NT,
        )
        if started:
            acc = acc + rest[0][...]
        if split is None:
            out_refs[0][...] = acc
        else:
            for m, ref in enumerate(out_refs):
                ref[...] = acc[m * split : (m + 1) * split, :].astype(BF16)

    if split is None:
        outs = [spec((total, width), F32)]
    else:
        outs = [spec((split, width))] * (total // split)
    return call(
        kernel,
        outs,
        [VMEM] * len(outs),
        [*units, *weights, *started],
        [VMEM] * (k + n + len(started)),
        (),
        after,
        2 * sum(u.shape[0] for u in units) * total * width * unit,
    )


def weight_grads(groups, unit, count, onto=(), after=()):
    pieces = [(i, *piece) for i, group in enumerate(groups) for piece in group[0]]
    units = [u for _, _, _, u in pieces]
    rows = [group[1] for group in groups]
    downs = [group[2] for group in groups]
    (total, width), k, n = rows[0].shape, len(pieces), len(groups)
    steps = [sum(u.shape[0] for i, _, _, u in pieces if downs[i] == d) for d in (False, True)]
    shapes = [(1, count * unit, width) if d else (1, width, count * unit) for d in downs]

    def kernel(*refs):
        u_refs, row_refs = refs[:k], refs[k : k + n]
        out_refs = refs[k + n + len(onto) :][:n]
        turned, across, along, sems = refs[-4:]
        source = None
        waits, used = [], [0, 0]
        for (i, block, first, _), u_ref in zip(pieces, u_refs):
            down = downs[i]
            if not down and source is not rows[i]:
                source = rows[i]
                turned[...] = row_refs[i][...].T
            for j in range(u_ref.shape[0]):
                at = pl.ds(pl.multiple_of(block(first + j) * unit, unit), unit)
                held = (along if down else across).at[used[down]]
                used[down] += 1
                if down:
                    held[...] = mm(u_ref[j, 0], row_refs[i][...], TN).astype(BF16)
                    target = out_refs[i].at[0, at, :]
                else:
                    held[...] = mm(turned[...], u_ref[j, 0]).astype(BF16)
                    target = out_refs[i].at[0, :, at]
                waits.append(pltpu.make_async_copy(held, target, sems.at[len(waits)]))
                waits[-1].start()
        for wait in waits:
            wait.wait()

    return call(
        kernel,
        [spec(shape) for shape in shapes],
        [ANY] * n,
        [*units, *rows, *onto],
        [VMEM] * (k + n) + [ANY] * len(onto),
        [
            pltpu.VMEM((width, total) if steps[0] else (8, 128), BF16),
            pltpu.VMEM((steps[0], width, unit) if steps[0] else (1, 8, 128), BF16),
            pltpu.VMEM((steps[1], unit, width) if steps[1] else (1, 8, 128), BF16),
            pltpu.SemaphoreType.DMA((sum(steps),)),
        ],
        after,
        2 * sum(steps) * total * width * unit,
        {k + n + i: n - len(onto) + i for i in range(len(onto))},
    )


def hop_orders(up, down):
    return (up, down), (up, down), (down, down), (down, up), (down, down)


def hypercube(tokens, gate_weights, expert_ids, w_gate, w_up, w_down, grad_out):
    members = lax.axis_size("expert")
    parts = lax.axis_size("tensor")
    bits = (parts // 2).bit_length() - 1
    count = tokens.shape[0]
    slot = 3 * count // (2 * members)
    unit = w_gate.shape[2] // parts
    half = parts // 2

    ids = expert_ids.reshape(1, count)
    gates = gate_weights.reshape(1, count)

    forward = tuple(range(bits))
    backward = forward[::-1]
    orders = dict(zip(("gu", "d", "h", "u", "g"), hop_orders(forward, backward)))

    def step_swap(x, step, name):
        pairs = [(d, d ^ (2 << orders[name][d % 2][step])) for d in range(parts)]
        return lax.ppermute(x, "tensor", pairs)

    def core_swap(x):
        return lax.ppermute(x, "tensor", [(d, d ^ 1) for d in range(parts)])

    def blocks_by(hops, other):
        def block(rel):
            t = lax.axis_index("tensor")
            core, chip = (t & 1) ^ other, t >> 1
            found = []
            for k in range(2):
                at = chip
                for step, bit in enumerate(hops[k]):
                    at = at ^ (((rel >> (bits - 1 - step)) & 1) << bit)
                index = jnp.int32(0)
                for bit in forward:
                    index = index * 2 + ((at >> bit) & 1)
                found.append(index)
            return half * core + jnp.where(core == 0, found[0], found[1])

        return block

    def halved(name):
        return blocks_by(orders[name], 0), blocks_by(orders[name], 1)

    def gathered(name):
        back = tuple(order[::-1] for order in orders[name])
        return blocks_by(back, 0), blocks_by(back, 1)

    def expert_swap(rows, skipped=0):
        out = []
        for m in range(1, members):
            pairs = [(d, d ^ m) for d in range(members)]
            out.append(lax.ppermute(rows[m - skipped], "expert", pairs))
        return out

    def halve(send, keep, name):
        size = send.shape[0]
        for step in range(bits):
            got = step_swap(send, step, name)
            total = keep + got.astype(F32)
            size //= 2
            if step < bits - 1:
                send, keep = total[size:].astype(BF16), total[:size]
        return total[0]

    def gather_units(x, name):
        for step in range(bits - 1):
            x = jnp.concatenate([x, step_swap(x, step, name)], axis=0)
        got = step_swap(x, bits - 1, name)
        mine, other = gathered(name)
        size = x.shape[0]
        early = ((mine, 0, x), (other, 0, core_swap(x)))
        late = ((mine, size, got), (other, size, core_swap(got)))
        return early, late

    x_slots, dy_slots = dispatch(ids, gates, tokens, grad_out, members, slot)
    x_rows = [x_slots[0]] + expert_swap(x_slots)
    weight_gate, weight_up, weight_down = load(
        (w_gate[0], w_up[0], w_down[0]), (x_slots[1],)
    )
    plain, gated = plan(ids, gates, members, slot, (weight_gate,))
    gate_up = (weight_gate, weight_up)
    dy_rows = [dy_slots[0]] + expert_swap(dy_slots)

    mine, other = halved("gu")
    away, x_all = away_terms(other, x_rows, gate_up, half, unit, False)
    send, keep = kept_terms(mine, x_all, gate_up, core_swap(away), unit, False)
    mine, other = halved("d")
    away, dy_all = away_terms(other, dy_rows, (weight_down,), half, unit, True, (send,))
    gate, up = halve(send, keep, "gu")
    send, keep = kept_terms(mine, dy_all, (weight_down,), core_swap(away), unit, True)
    (d_hidden,) = halve(send, keep, "d")

    hidden = (gate * jax.nn.sigmoid(gate) * up).astype(BF16)
    hidden, gate, up = lax.optimization_barrier((hidden, gate, up))
    sigma = jax.nn.sigmoid(gate)
    active = gate * sigma
    d_gate = (d_hidden * up * sigma * (1.0 + gate * (1.0 - sigma))).astype(BF16)
    d_up = (d_hidden * active).astype(BF16)

    hidden_early, hidden_late = gather_units(hidden[None, None], "h")
    up_early, up_late = gather_units(d_up[None, None], "u")
    gate_early, gate_late = gather_units(d_gate[None, None], "g")
    gate_all = gate_early + gate_late

    (part,) = unit_rows(((weight_down, hidden_early),), unit, True)
    out = unit_rows(((weight_down, hidden_late),), unit, True, part, slot)
    out_back = expert_swap(out)
    grad_w_down = weight_grads(((hidden_early, dy_all, True),), unit, parts)
    (part,) = unit_rows(((weight_up, up_early),), unit, False)
    (part,) = unit_rows(((weight_up, up_late), (weight_gate, gate_early)), unit, False, part)
    back = unit_rows(((weight_gate, gate_late),), unit, False, part, slot)
    grad_back = expert_swap(back)
    grad_w_up = weight_grads(((up_early, x_all, False),), unit, parts)
    grad_w_gate, grad_w_up, grad_w_down = weight_grads(
        ((gate_all, x_all, False), (up_late, x_all, False), (hidden_late, dy_all, True)),
        unit,
        parts,
        (*grad_w_up, *grad_w_down),
    )
    mixed, grad_tokens = collect(
        (gated, plain), ([out[0]] + out_back, [back[0]] + grad_back)
    )
    return (mixed, grad_tokens, grad_w_gate, grad_w_up, grad_w_down)


def power_of_two(n):
    return n & (n - 1) == 0


def solution(mesh):
    members, parts = mesh.shape["expert"], mesh.shape["tensor"]

    def local(*args):
        unit = args[3].shape[2] // parts
        slot = 3 * args[0].shape[0] // (2 * members)
        fits = power_of_two(members) and power_of_two(parts) and parts >= 4
        fits = fits and unit % 128 == 0 and slot % 16 == 0 and args[0].shape[1] % 128 == 0
        fits = fits and args[2].shape[1] == 1
        return (hypercube if fits else general)(*args)

    in_specs = (
        P("expert", "tensor"),
        P("expert", None),
        P("expert", None),
        P("expert", "tensor", None),
        P("expert", "tensor", None),
        P("expert", None, "tensor"),
        P("expert", "tensor"),
    )
    out_specs = (
        P("expert", "tensor"),
        P("expert", "tensor"),
        P("expert", "tensor", None),
        P("expert", "tensor", None),
        P("expert", None, "tensor"),
    )
    return jax.shard_map(local, mesh=mesh, in_specs=in_specs, out_specs=out_specs, check_vma=False)
```
